32 devices in a mesh: section: 8 (over y, x, core), tensor: 4 (over z).
Axes of the slice: x: 2, y: 2, z: 4, core: 2. Of those that a mesh axis runs over, the one named last changes fastest.
Arguments:
- acts: bfloat16 [8, 2, 32, 4096], P('section', None, None, 'tensor'), may hold values from -6 to 6
- grads_in: bfloat16 [8, 2, 32, 4096], P('section', None, None, 'tensor'), may hold values from -6 to 6
- head_grads: bfloat16 [8, 2, 128, 512], P('section', None, None, 'tensor'), may hold values from -6 to 6
- types: int32 [8, 2, 32], P('section'), may hold values 0 or 1
- gains: bfloat16 [8, 2, 2, 1024], P('section'), may hold values from 0.3984375 to 1.59375
- w_query: bfloat16 [8, 2, 4096, 512], P('section', None, None, 'tensor'), may hold values from -0.09375 to 0.09375
- w_key: bfloat16 [8, 2, 4096, 128], P('section', None, None, 'tensor'), may hold values from -0.09375 to 0.09375
- w_value: bfloat16 [8, 2, 4096, 128], P('section', None, None, 'tensor'), may hold values from -0.09375 to 0.09375
Outputs:
- routed: bfloat16 [8, 2, 32, 4096], P('section', None, None, 'tensor')
The draws below stay inside these ranges and needn't reach their ends.
All inputs are finite; a program needn't handle non-finite values. No bound on the sum of `types` on one device may be relied on, other than what follows from the above.
Results may differ from the reference program's by a relative error of at most 0.0055.
Values may be sent and summed in bfloat16 or wider, within the bound.
A program may use at most 64 MiB of HBM per device.

```python
import jax
import jax.numpy as jnp
from jax import lax

D = 4096
HEAD_DIM = 128
SUB = 4
SPANS = 2
TOK = 128
TOKQ = 32
N_SECTION = 8
N_TENSOR = 4


def set_ends(values, stream_key, smallest, top_value):
    longest = values.shape.index(max(values.shape))
    spots = []
    for shift in (0, 1):
        where = [jax.random.randint(jax.random.fold_in(stream_key, axis), (), 0, length) for axis, length in enumerate(values.shape)]
        where[longest] = (where[longest] + shift) % values.shape[longest]
        spots.append(tuple(where))
    return values.at[spots[0]].set(smallest).at[spots[1]].set(top_value)


def block_scale(own_key, shape, cuts, least, high):
    def one(dim, parts):
        steps = jax.random.uniform(jax.random.fold_in(jax.random.fold_in(own_key, 6), dim), (parts,), jnp.float32, least / len(cuts), high / len(cuts))
        return jnp.repeat(jnp.exp(steps), shape[dim] // parts).reshape((-1,) + (1,) * (len(shape) - dim - 1))

    gain = one(*cuts[0])
    for cut in cuts[1:]:
        gain = gain * one(*cut)
    return gain


def bell_draw(rng, dims, width, most, split=(), held_as=jnp.bfloat16):
    values = jax.random.normal(rng, dims, jnp.float32) * width
    if len(split) > 0:
        values = block_scale(rng, dims, split, -0.22, 0.18) * values
    return jnp.clip(values, min=-most, max=most).astype(held_as)


def setup_inputs(seed: int = 0) -> dict:
    keys = jax.random.split(jax.random.key(seed), 9)
    acts = bell_draw(keys[0], (N_SECTION, SPANS, TOKQ, D), 1.0, 6.0, ((0, 8), (3, 4)))
    grads_in = bell_draw(keys[1], (N_SECTION, SPANS, TOKQ, D), 1.0, 6.0, ((0, 8), (3, 4)))
    head_grads = bell_draw(keys[2], (N_SECTION, SPANS, TOK, HEAD_DIM * N_TENSOR), 1.0, 6.0, ((0, 8), (3, 4)))
    types = set_ends((jax.random.randint(keys[3], (N_SECTION, SPANS, TOKQ), 0, 2) < 1).astype(jnp.int32), jax.random.fold_in(keys[3], 1), 0, 1)
    gains = jnp.clip(1.0 + 0.12 * jax.random.normal(keys[4], (N_SECTION, SPANS, 2, D // SUB), jnp.float32), 0.3984375, 1.59375).astype(jnp.bfloat16)
    w_query = bell_draw(keys[5], (N_SECTION, SPANS, D, HEAD_DIM * N_TENSOR), D ** -0.5, 0.09375, ((0, 8), (3, 4)))
    w_key = bell_draw(keys[6], (N_SECTION, SPANS, D, HEAD_DIM), D ** -0.5, 0.09375, ((0, 8), (3, 4)))
    w_value = bell_draw(keys[7], (N_SECTION, SPANS, D, HEAD_DIM), D ** -0.5, 0.09375, ((0, 8), (3, 4)))
    return dict(acts=acts, grads_in=grads_in, head_grads=head_grads, types=types, gains=gains, w_query=w_query, w_key=w_key, w_value=w_value)


epsilon = 1e-05

def span_backward(inputs):
    x_rows, grad_rows, kind_rows, gain_pair, w_query, w_key, w_value, head_rows = inputs
    heads = w_query.shape[1] // HEAD_DIM
    groups = w_key.shape[1] // HEAD_DIM
    per_group = heads // groups
    tokens = x_rows.shape[0]
    x_float = x_rows.astype(jnp.float32)
    inverse = lax.rsqrt(lax.optimization_barrier(jnp.mean(x_float * x_float, axis=-1, keepdims=True)) + epsilon)
    gain_rows = jnp.where(kind_rows[:, None] == 1, gain_pair[1][None, :], gain_pair[0][None, :]).astype(jnp.float32)
    normed = (x_float * inverse * gain_rows).astype(jnp.bfloat16)
    queries = jnp.dot(normed, w_query, preferred_element_type=jnp.float32).astype(jnp.bfloat16).reshape(tokens, heads, HEAD_DIM)
    key_rows = jnp.dot(normed, w_key, preferred_element_type=jnp.float32).astype(jnp.bfloat16).reshape(tokens, groups, HEAD_DIM)
    value_rows = jnp.dot(normed, w_value, preferred_element_type=jnp.float32).astype(jnp.bfloat16).reshape(tokens, groups, HEAD_DIM)
    key_heads = jnp.repeat(key_rows, per_group, axis=1).astype(jnp.float32)
    value_heads = jnp.repeat(value_rows, per_group, axis=1).astype(jnp.float32)
    query_float = queries.astype(jnp.float32)
    softmax_scale = HEAD_DIM ** (-0.5)
    scores = jnp.einsum('qhd,khd->hqk', query_float, key_heads) * softmax_scale
    causal = jnp.arange(tokens)[:, None] >= jnp.arange(tokens)[None, :]
    scores = jnp.where(causal[None], scores, -1e+30)
    attn_probs = jax.nn.softmax(scores, axis=-1)
    probs_low = attn_probs.astype(jnp.bfloat16)
    out_float = head_rows.reshape(tokens, heads, HEAD_DIM).astype(jnp.float32)
    prob_grads = jnp.einsum('qhd,khd->hqk', out_float, value_heads)
    score_grads = (attn_probs * (prob_grads - lax.optimization_barrier(jnp.sum(prob_grads * attn_probs, axis=-1, keepdims=True))) * softmax_scale).astype(jnp.bfloat16)
    score_float = score_grads.astype(jnp.float32)
    query_grads = jnp.einsum('hqk,khd->qhd', score_float, key_heads).astype(jnp.bfloat16)
    key_each = jnp.einsum('hqk,qhd->khd', score_float, query_float)
    value_each = jnp.einsum('hqk,qhd->khd', probs_low.astype(jnp.float32), out_float)
    key_grads = key_each.reshape(tokens, groups, per_group, HEAD_DIM).sum(axis=2).astype(jnp.bfloat16)
    value_grads = value_each.reshape(tokens, groups, per_group, HEAD_DIM).sum(axis=2).astype(jnp.bfloat16)
    partial_value = jnp.dot(query_grads.reshape(tokens, heads * HEAD_DIM), w_query.T, preferred_element_type=jnp.float32)
    partial_value = partial_value + jnp.dot(key_grads.reshape(tokens, groups * HEAD_DIM), w_key.T, preferred_element_type=jnp.float32)
    partial_value = partial_value + jnp.dot(value_grads.reshape(tokens, groups * HEAD_DIM), w_value.T, preferred_element_type=jnp.float32)
    stat_mean = lax.optimization_barrier(jnp.mean(x_float * gain_rows * partial_value, axis=-1, keepdims=True))
    norm_grads = inverse * gain_rows * partial_value - x_float * inverse ** 3 * stat_mean
    return (grad_rows.astype(jnp.float32) + norm_grads).astype(jnp.bfloat16)

def rows_join(array):
    sections = N_SECTION // SUB
    shaped = array.reshape((sections, SUB) + array.shape[1:])
    shaped = jnp.swapaxes(shaped, 1, 2)
    return shaped.reshape((sections * SPANS, SUB * array.shape[2]) + array.shape[3:])

def cols_join(array):
    sections = N_SECTION // SUB
    shaped = array.reshape((sections, SUB) + array.shape[1:])
    shaped = jnp.moveaxis(shaped, 1, -2)
    return shaped.reshape((sections * SPANS,) + array.shape[2:-1] + (SUB * array.shape[-1],))

def reference(acts, grads_in, head_grads, types, gains, w_query, w_key, w_value):
    sections = N_SECTION // SUB
    inputs = (rows_join(acts), rows_join(grads_in), rows_join(types), cols_join(gains), cols_join(w_query), cols_join(w_key), cols_join(w_value), cols_join(head_grads))
    results = lax.map(span_backward, inputs)
    results = results.reshape(sections, SPANS, TOK, D)
    rolled = jnp.roll(results, -1, axis=0)
    rolled = rolled.at[sections - 1].set(results[0][::-1])
    shaped = rolled.reshape(sections, SPANS, SUB, TOK // SUB, D)
    shaped = jnp.swapaxes(shaped, 1, 2)
    return shaped.reshape(N_SECTION, SPANS, TOK // SUB, D)
```

```python
import jax
import jax.numpy as jnp
from jax import lax
from jax.experimental import pallas as pl
from jax.experimental.pallas import tpu as pltpu
from jax.sharding import PartitionSpec as P

SUB = 4
EPS = 1e-05
MESH = pl.DeviceIdType.MESH
F32 = jnp.float32
BF16 = jnp.bfloat16
ACROSS, PAIR, PAIR_X, NEAR, FAR, NEAR_R, FAR_R = range(7)


def dot(a, b, dims):
    return lax.dot_general(a, b, (dims, ((), ())), preferred_element_type=F32)


def kernel(
    sections, tensors,
    acts, grads, heads, types, gains, wq, wk, wv,
    out,
    xg, kinds, gain_all, wkv, wvv, wcat, hg, gr, kindc, invc, acc, square,
    kvt, dkv, dkv_in, stat, stat_z, stat_s, stat_in,
    part, part_in, xs, xr, zs, zr,
    loc, ag_s, ag_r, small_s, small_r, kv_s, kv_r, dk_s, dk_r, st_s, st_r, sp_s, sp_r,
    pair_s, pair_r, x_s, x_r, z_s, z_r,
):
    spans, rows, cols = acts.shape
    n = SUB * rows
    hd = wq.shape[3]
    kc = wk.shape[1]
    width = cols * tensors
    gcols = gains.shape[2]
    T = tensors
    t = lax.axis_index("tensor")
    sec = lax.axis_index("section")
    pos = lax.rem(sec, SUB)
    here = sec // SUB
    base = here * SUB
    xi = pos // 2
    ci = lax.rem(pos, 2)
    pos_pair = xi * 2 + (1 - ci)
    pos_x = (1 - xi) * 2 + ci
    pos_diag = (1 - xi) * 2 + (1 - ci)
    pair_dev = (base + pos_pair, t)
    x_dev = (base + pos_x, t)
    section_before = lax.rem(here + sections - 1, sections)
    section_after = lax.rem(here + 1, sections)
    before = section_before * SUB + pos
    after = section_after * SUB + pos

    both = 2 * lax.min(t, T - 1 - t)
    order = [t]
    for j in range(1, T):
        d = (j + 1) // 2
        near = t - d if j % 2 else t + d
        rest = lax.select(2 * t < T - 1, jnp.int32(j), jnp.int32(T - 1 - j))
        order.append(lax.select(j <= both, near, rest))

    def pos_peer(k):
        return (base + lax.rem(pos + k, SUB), t)

    def z_peer(k):
        return (sec, lax.rem(t + k, T))

    def send(src, dst, ssem, rsem, dev):
        pltpu.make_async_remote_copy(
            src_ref=src, dst_ref=dst, send_sem=ssem, recv_sem=rsem, device_id=dev, device_id_type=MESH
        ).start()

    def sent(src, ssem):
        pltpu.make_async_copy(src, src, ssem).wait()

    def arrived(dst, rsem):
        pltpu.make_async_copy(dst, dst, rsem).wait()

    def rowpos(p):
        return pl.ds(pl.multiple_of(p * rows, rows), rows)

    def blk(v, p, tt):
        return xg.at[v, tt, rowpos(p), :]

    own = [pltpu.make_async_copy(acts.at[v], blk(v, pos, t), loc.at[v]) for v in range(2)]
    kload = pltpu.make_async_copy(types, kinds.at[pos], loc.at[2])
    gload = pltpu.make_async_copy(gains, gain_all.at[pos], loc.at[3])
    wload = [
        pltpu.make_async_copy(wk, wkv, loc.at[5]),
        pltpu.make_async_copy(wv, wvv, loc.at[6]),
    ]
    qload = pltpu.make_async_copy(wq, wcat.at[:, :, :, pl.ds(0, hd)], loc.at[4])
    hload = pltpu.make_async_copy(heads, hg, loc.at[7])
    grload = pltpu.make_async_copy(grads, gr, loc.at[8])
    for copy in own[::-1] + [kload, gload] + wload + [qload, hload, grload]:
        copy.start()

    barrier = pltpu.get_barrier_semaphore()
    greeted = [z_peer(k) for k in range(1, T)] + [pos_peer(k) for k in range(1, SUB)]
    greeted += [(before, lax.rem(t + k, T)) for k in range(T)]
    greeted += [(after, lax.rem(t + k, T)) for k in range(T)]
    for dev in greeted:
        pl.semaphore_signal(barrier, inc=1, device_id=dev, device_id_type=MESH)
    pl.semaphore_wait(barrier, len(greeted))

    def pass_block(v, p, tt, kind, dev):
        send(blk(v, p, tt), blk(v, p, tt), ag_s.at[v, kind, tt], ag_r.at[v, p, tt], dev)

    def ag_wait(v, p, tt):
        arrived(blk(v, p, tt), ag_r.at[v, p, tt])

    def own_ways():
        for kind, step in ((NEAR, -1), (NEAR_R, 1), (FAR, -2), (FAR_R, 2)):
            goal = t + step
            inside = goal >= 0 if step < 0 else goal < T
            yield kind, inside, (sec, lax.min(lax.max(goal, 0), T - 1))

    def along(v):
        for kind, inside, dev in own_ways():

            @pl.when(inside)
            def _():
                pass_block(v, pos, t, kind, dev)

    def onward_ways(j):
        if not any(d % 2 == 0 for d in range((j + 1) // 2, j + 1)):
            return
        tt = order[j]
        away = lax.select(tt < t, jnp.int32(1), jnp.int32(-1))
        even = lax.rem((t - tt) * away, 2) == 0
        for kind, step in ((NEAR, 1), (FAR, 2)):
            if T <= 2 + step:
                continue
            goal = t + step * away
            use = jnp.logical_and(even, jnp.logical_and(goal >= 0, goal < T))
            yield kind, use, (sec, lax.min(lax.max(goal, 0), T - 1))

    def take(v, j):
        tt = order[j]
        ag_wait(v, pos, tt)
        for kind, use, dev in onward_ways(j):

            @pl.when(use)
            def _():
                pass_block(v, pos, tt, kind, dev)

        pass_block(v, pos, tt, ACROSS, x_dev)
        pass_block(v, pos, tt, PAIR, pair_dev)

    def take_x(v, j):
        ag_wait(v, pos_x, order[j])
        pass_block(v, pos_x, order[j], PAIR_X, pair_dev)

    own[1].wait()
    pass_block(1, pos, t, ACROSS, x_dev)
    along(1)
    pass_block(1, pos, t, PAIR, pair_dev)
    kload.wait()
    gload.wait()
    for k in range(1, SUB):
        send(kinds.at[pos], kinds.at[pos], small_s.at[0, k], small_r.at[0, k], pos_peer(k))
        send(gain_all.at[pos], gain_all.at[pos], small_s.at[1, k], small_r.at[1, k], pos_peer(k))
    own[0].wait()
    pass_block(0, pos, t, ACROSS, x_dev)
    pass_block(0, pos, t, PAIR, pair_dev)

    for copy in wload:
        copy.wait()
    qload.wait()

    def join_weights(v):
        for i in range(T):
            at = pl.ds(i * cols, cols)
            kv_cols = jnp.concatenate([wkv[v, :, at], wvv[v, :, at]], axis=0)
            wcat[v, i, :, hd:] = jnp.transpose(kv_cols)

    def project(v, j):
        tt = order[j]
        for p in (pos_pair, pos_diag):
            ag_wait(v, p, tt)
        block = tt * cols // gcols
        off = pl.multiple_of(lax.rem(tt * cols, gcols), cols)
        speech = kindc[v, :, 0:1] > 0.5
        pair = gain_all[block, v, :, pl.ds(off, cols)].astype(F32)
        xf = xg[v, tt].astype(F32)
        squares = jnp.broadcast_to(jnp.sum(xf * xf, axis=1, keepdims=True), (n, 128))
        scaled = (xf * jnp.where(speech, pair[1:2, :], pair[0:1, :])).astype(BF16)
        product = dot(scaled, wcat[v, tt], ((1,), (0,)))
        if j == 0:
            square[v] = squares
            acc[v] = product
        else:
            square[v] += squares
            acc[v] += product

    mine = pl.ds(pl.multiple_of(t * kc, kc), kc)
    queries = [None, None]

    def share_keys(v):
        inverse = lax.rsqrt(square[v][:, 0:1] / width + EPS)
        invc[v] = jnp.broadcast_to(inverse, (n, 128))
        projected = acc[v] * inverse
        turned = jnp.transpose(projected[:, hd:]).astype(BF16)
        kvt[v, 0, mine, :] = turned[:kc]
        kvt[v, 1, mine, :] = turned[kc:]
        for k in range(1, T):
            block = kvt.at[v, :, mine, :]
            send(block, block, kv_s.at[v, k], kv_r.at[v, k], z_peer(k))
        queries[v] = projected[:, :hd].astype(BF16)

    scale = hd ** (-0.5)
    query_grads = [None, None]

    def attend(v):
        eye = lax.broadcasted_iota(jnp.int32, (n, n), 0) == lax.broadcasted_iota(jnp.int32, (n, n), 1)
        causal = lax.broadcasted_iota(jnp.int32, (n, n), 0) >= lax.broadcasted_iota(
            jnp.int32, (n, n), 1
        )
        for k in range(1, T):
            source = lax.rem(t - k + T, T)
            theirs = kvt.at[v, :, pl.ds(pl.multiple_of(source * kc, kc), kc), :]
            arrived(theirs, kv_r.at[v, k])
        kt = kvt[v, 0]
        vt = kvt[v, 1]
        og = hg[v]
        scores = dot(queries[v], kt, ((1,), (0,))) * scale
        scores = jnp.where(causal, scores, -1e30)
        top = jnp.max(scores, axis=1, keepdims=True)
        weights = jnp.exp(scores - top)
        probs = weights / jnp.sum(weights, axis=1, keepdims=True)
        pg = dot(og, vt, ((1,), (0,)))
        sg = probs * (pg - jnp.sum(pg * probs, axis=1, keepdims=True)) * scale
        sg = sg.astype(BF16)
        key_each = dot(queries[v], sg, ((0,), (0,)))
        value_each = dot(og, probs.astype(BF16), ((0,), (0,)))
        dkv[v, 0] = key_each.astype(BF16)
        dkv[v, 1] = value_each.astype(BF16)
        for k in range(1, T):
            goal = pl.ds(pl.multiple_of(lax.rem(t + k, T) * kc, kc), kc)
            send(dkv.at[v, :, goal, :], dkv_in.at[k - 1, v], dk_s.at[v, k], dk_r.at[v, k], z_peer(k))
        qg = dot(sg, kt, ((1,), (1,)))
        query_grads[v] = qg.astype(BF16)
        column = jnp.sum(qg * queries[v].astype(F32), axis=1, keepdims=True)
        line = jnp.sum(jnp.where(eye, column, 0.0), axis=0, keepdims=True)
        line = line + jnp.sum(
            key_each * kt.astype(F32) + value_each * vt.astype(F32), axis=0, keepdims=True
        )
        stat[v] = jnp.broadcast_to(line, (8, n))
        for k in range(1, T):
            send(stat.at[v], stat_z.at[v, k - 1], st_s.at[v, k], st_r.at[v, k], z_peer(k))

    def share_stat(v):
        line = stat[v]
        for k in range(1, T):
            arrived(stat_z.at[v, k - 1], st_r.at[v, k])
            line = line + stat_z[v, k - 1]
        stat_s[v] = line
        for k in range(1, SUB):
            send(stat_s.at[v], stat_in.at[v, k - 1], sp_s.at[v, k], sp_r.at[v, k], pos_peer(k))

    def joined_grads(v):
        summed = dkv[v, :, mine, :].astype(F32)
        for k in range(1, T):
            arrived(dkv_in.at[k - 1, v], dk_r.at[v, k])
            summed = summed + dkv_in[k - 1, v].astype(F32)
        kv_rows = jnp.transpose(summed.reshape(2 * kc, n)).astype(BF16)
        return jnp.concatenate([query_grads[v], kv_rows], axis=1)

    def term(v, joined, j):
        i = order[j]
        piece = dot(joined, wcat[v, i], ((1,), (1,))).astype(BF16)
        for p in range(SUB):
            part[v, i, p % 2, p // 2] = piece[p * rows : (p + 1) * rows]
        send(part.at[v, i, 1 - ci], part_in.at[v, i], pair_s.at[v, i], pair_r.at[v, i], pair_dev)

    def cross(v, j):
        i = order[j]
        arrived(part_in.at[v, i], pair_r.at[v, i])
        xs[v, i] = (part[v, i, ci, 1 - xi].astype(F32) + part_in[v, i, 1 - xi].astype(F32)).astype(BF16)
        send(xs.at[v, i], xr.at[v, i], x_s.at[v, i], x_r.at[v, i], x_dev)

    def slot(v, section):
        return lax.select(section == 0, jnp.int32(1 - v), jnp.int32(v))

    def deliver(v, j):
        i = order[j]
        arrived(xr.at[v, i], x_r.at[v, i])
        summed = (
            part[v, i, ci, xi].astype(F32) + part_in[v, i, xi].astype(F32) + xr[v, i].astype(F32)
        )
        inverse = invc[v, rowpos(pos), 0:1]
        speech = kindc[v, rowpos(pos), 0:1] > 0.5
        off = pl.multiple_of(lax.rem(i * cols, gcols), cols)
        pair = gain_all[i * cols // gcols, v, :, pl.ds(off, cols)].astype(F32)
        summed = inverse * jnp.where(speech, pair[1:2, :], pair[0:1, :]) * summed
        if j == 0:
            line = stat_s[v]
            for k in range(1, SUB):
                arrived(stat_in.at[v, k - 1], sp_r.at[v, k])
                line = line + stat_in[v, k - 1]
            lane = lax.broadcasted_iota(jnp.int32, (rows, n), 1)
            row = lax.broadcasted_iota(jnp.int32, (rows, n), 0)
            pick = lane == row + pos * rows
            mean = jnp.sum(jnp.where(pick, line[0:1, :], 0.0), axis=1, keepdims=True) / width
            x = xg[v, t, rowpos(pos), :].astype(F32)
            summed = gr[v].astype(F32) + summed - x * (inverse * inverse * mean)
        zs[v, i] = summed.astype(BF16)
        goal = slot(v, here)
        send(zs.at[v, i], zr.at[goal, t], z_s.at[v, i], z_r.at[goal, t], (before, i))

    def collect(v):
        goal = slot(v, section_after)
        total = None
        for j in range(T - 1, -1, -1):
            arrived(zr.at[goal, order[j]], z_r.at[goal, order[j]])
        for i in range(T):
            theirs = zr[goal, i].astype(F32)
            total = theirs if total is None else total + theirs
        out[goal] = total.astype(BF16)

    def read_kinds():
        eye_r = lax.broadcasted_iota(jnp.int32, (rows, rows), 0) == lax.broadcasted_iota(
            jnp.int32, (rows, rows), 1
        )
        for j in range(1, SUB):
            source = lax.rem(pos - j + SUB, SUB)
            arrived(kinds.at[source], small_r.at[0, j])
            arrived(gain_all.at[source], small_r.at[1, j])
        for v in range(2):
            for p in range(SUB):
                line = kinds[p, v : v + 1, :].astype(F32)
                column = jnp.sum(jnp.where(eye_r, line, 0.0), axis=1, keepdims=True)
                kindc[v, p * rows : (p + 1) * rows, :] = jnp.broadcast_to(column, (rows, 128))

    join_weights(1)
    take(1, 1)
    along(0)
    take_x(1, 0)
    read_kinds()
    project(1, 0)
    for j in range(2, T):
        take(1, j)
        take_x(1, j - 1)
        project(1, j - 1)
    take(0, 1)
    take_x(0, 0)
    take_x(1, T - 1)
    project(1, T - 1)
    share_keys(1)
    join_weights(0)
    project(0, 0)
    for j in range(2, T):
        take(0, j)
        take_x(0, j - 1)
        project(0, j - 1)
    hload.wait()
    attend(1)
    take_x(0, T - 1)
    project(0, T - 1)
    share_keys(0)
    share_stat(1)
    joined = joined_grads(1)
    for j in range(T - 1, -1, -1):
        term(1, joined, j)
        if j < T - 1:
            cross(1, j + 1)
    cross(1, 0)
    attend(0)
    grload.wait()
    for j in range(T - 1, -1, -1):
        deliver(1, j)
    share_stat(0)
    joined = joined_grads(0)
    for j in range(T - 1, -1, -1):
        term(0, joined, j)
        if j < T - 1:
            cross(0, j + 1)
    cross(0, 0)
    for j in range(T - 1, -1, -1):
        deliver(0, j)

    for v in range(2):
        for kind, inside, dev in own_ways():

            @pl.when(inside)
            def _():
                sent(blk(v, pos, t), ag_s.at[v, kind, t])

        for j in range(T):
            for p, kind in ((pos, ACROSS), (pos, PAIR), (pos_x, PAIR_X)):
                sent(blk(v, p, order[j]), ag_s.at[v, kind, order[j]])
            if j > 0:
                for kind, use, dev in onward_ways(j):

                    @pl.when(use)
                    def _():
                        sent(blk(v, pos, order[j]), ag_s.at[v, kind, order[j]])

        for k in range(1, SUB):
            sent(stat_s.at[v], sp_s.at[v, k])
        for k in range(1, T):
            goal = pl.ds(pl.multiple_of(lax.rem(t + k, T) * kc, kc), kc)
            sent(kvt.at[v, :, mine, :], kv_s.at[v, k])
            sent(dkv.at[v, :, goal, :], dk_s.at[v, k])
            sent(stat.at[v], st_s.at[v, k])
        for i in range(T):
            sent(part.at[v, i, 1 - ci], pair_s.at[v, i])
            sent(xs.at[v, i], x_s.at[v, i])
            sent(zs.at[v, i], z_s.at[v, i])
    for k in range(1, SUB):
        sent(kinds.at[pos], small_s.at[0, k])
        sent(gain_all.at[pos], small_s.at[1, k])
    collect(1)
    collect(0)


def per_device(sections, acts, grads_in, head_grads, types, gains, w_query, w_key, w_value):
    T = lax.axis_size("tensor")
    acts, grads_in, head_grads, types, gains = acts[0], grads_in[0], head_grads[0], types[0], gains[0]
    w_query, w_key, w_value = w_query[0], jnp.swapaxes(w_key[0], 1, 2), jnp.swapaxes(w_value[0], 1, 2)
    spans, rows, cols = acts.shape
    n = SUB * rows
    hd = w_query.shape[2]
    kc = w_key.shape[1]
    w_query = w_query.reshape(spans, T, cols, hd)
    V = pltpu.VMEM
    D = pltpu.SemaphoreType.DMA
    scratch = [
        V((2, T, n, cols), BF16), V((SUB, 2, rows), jnp.int32), V((SUB,) + gains.shape, BF16),
        V(w_key.shape, BF16), V(w_value.shape, BF16),
        V((2, T, cols, hd + 2 * kc), BF16), V(head_grads.shape, BF16), V(grads_in.shape, BF16),
        V((2, n, 128), F32), V((2, n, 128), F32), V((2, n, hd + 2 * kc), F32), V((2, n, 128), F32),
        V((2, 2, hd, n), BF16), V((2, 2, hd, n), BF16), V((T - 1, 2, 2, kc, n), BF16),
        V((2, 8, n), F32), V((2, T - 1, 8, n), F32), V((2, 8, n), F32), V((2, SUB - 1, 8, n), F32),
        V((2, T, 2, 2, rows, cols), BF16), V((2, T, 2, rows, cols), BF16),
        V((2, T, rows, cols), BF16), V((2, T, rows, cols), BF16),
        V((2, T, rows, cols), BF16), V((2, T, rows, cols), BF16),
        D((9,)), D((2, 7, T)), D((2, SUB, T)), D((2, SUB)), D((2, SUB)),
        D((2, T)), D((2, T)), D((2, T)), D((2, T)), D((2, T)), D((2, T)), D((2, SUB)), D((2, SUB)),
        D((2, T)), D((2, T)), D((2, T)), D((2, T)), D((2, T)), D((2, T)),
    ]

    def body(*refs):
        kernel(sections, T, *refs)

    routed = pl.pallas_call(
        body,
        out_shape=jax.ShapeDtypeStruct((2, rows, cols), BF16),
        in_specs=[pl.BlockSpec(memory_space=pl.ANY)] * 8,
        out_specs=pl.BlockSpec(memory_space=pltpu.VMEM),
        scratch_shapes=scratch,
        compiler_params=pltpu.CompilerParams(
            collective_id=0, has_side_effects=True, vmem_limit_bytes=67_000_000
        ),
        name="relay",
    )(acts, grads_in, head_grads, types, gains, w_query, w_key, w_value)
    return routed[None]


def solution(mesh):
    sections = mesh.shape["section"] // SUB

    def run(*args):
        return per_device(sections, *args)

    return jax.shard_map(
        run,
        mesh=mesh,
        in_specs=(
            P("section", None, None, "tensor"),
            P("section", None, None, "tensor"),
            P("section", None, None, "tensor"),
            P("section", None, None),
            P("section", None, None, None),
            P("section", None, None, "tensor"),
            P("section", None, None, "tensor"),
            P("section", None, None, "tensor"),
        ),
        out_specs=P("section", None, None, "tensor"),
        check_vma=False,
    )
```

```python
import jax
import jax.numpy as jnp
from jax import lax
from jax.experimental import pallas as pl
from jax.experimental.pallas import tpu as pltpu
from jax.sharding import PartitionSpec as P

SUB = 4
EPS = 1e-05
MESH = pl.DeviceIdType.MESH
F32 = jnp.float32
BF16 = jnp.bfloat16
ACROSS, PAIR, PAIR_X, NEAR, FAR, NEAR_R, FAR_R, NEAR_X, NEAR_XR = range(9)
FROM_Z, FROM_X, FROM_PAIR = range(3)


def dot(a, b, dims):
    return lax.dot_general(a, b, (dims, ((), ())), preferred_element_type=F32)


def kernel(
    sections, tensors,
    acts, grads, heads, types, gains, wq, wk, wv,
    out,
    xg, kinds, gain_all, wkv, wvv, wcat, hg, gr, kindc, invc, acc, square,
    kvt, dkv, dkv_in, stat, stat_z, stat_s, stat_in,
    part, part_in, xs, xr, zs, zr,
    loc, ag_s, far_s, relay_s, ag_r, small_s, small_r, kv_s, kv_r, dk_s, dk_r, st_s, st_r, sp_s, sp_r,
    pair_s, pair_r, x_s, x_r, z_s, z_r,
):
    spans, rows, cols = acts.shape
    n = SUB * rows
    hd = wq.shape[3]
    kc = wk.shape[1]
    width = cols * tensors
    gcols = gains.shape[2]
    T = tensors
    t = lax.axis_index("tensor")
    sec = lax.axis_index("section")
    pos = lax.rem(sec, SUB)
    here = sec // SUB
    base = here * SUB
    xi = pos // 2
    ci = lax.rem(pos, 2)
    pos_pair = xi * 2 + (1 - ci)
    pos_x = (1 - xi) * 2 + ci
    pos_diag = (1 - xi) * 2 + (1 - ci)
    pair_dev = (base + pos_pair, t)
    x_dev = (base + pos_x, t)
    section_before = lax.rem(here + sections - 1, sections)
    section_after = lax.rem(here + 1, sections)
    before = section_before * SUB + pos
    after = section_after * SUB + pos

    both = 2 * lax.min(t, T - 1 - t)
    order = [t]
    for j in range(1, T):
        d = (j + 1) // 2
        near = t - d if j % 2 else t + d
        rest = lax.select(2 * t < T - 1, jnp.int32(j), jnp.int32(T - 1 - j))
        order.append(lax.select(j <= both, near, rest))

    def pos_peer(k):
        return (base + lax.rem(pos + k, SUB), t)

    def z_peer(k):
        return (sec, lax.rem(t + k, T))

    def send(src, dst, ssem, rsem, dev):
        pltpu.make_async_remote_copy(
            src_ref=src, dst_ref=dst, send_sem=ssem, recv_sem=rsem, device_id=dev, device_id_type=MESH
        ).start()

    def sent(src, ssem):
        pltpu.make_async_copy(src, src, ssem).wait()

    def arrived(dst, rsem):
        pltpu.make_async_copy(dst, dst, rsem).wait()

    def rowpos(p):
        return pl.ds(pl.multiple_of(p * rows, rows), rows)

    def blk(v, p, tt):
        return xg.at[v, tt, rowpos(p), :]

    own = [pltpu.make_async_copy(acts.at[v], blk(v, pos, t), loc.at[v]) for v in range(2)]
    kload = pltpu.make_async_copy(types, kinds.at[pos], loc.at[2])
    gload = pltpu.make_async_copy(gains, gain_all.at[pos], loc.at[3])
    wload = [
        pltpu.make_async_copy(wk, wkv, loc.at[5]),
        pltpu.make_async_copy(wv, wvv, loc.at[6]),
    ]
    qload = pltpu.make_async_copy(wq, wcat.at[:, :, :, pl.ds(0, hd)], loc.at[4])
    hload = pltpu.make_async_copy(heads, hg, loc.at[7])
    grload = pltpu.make_async_copy(grads, gr, loc.at[8])
    for copy in own[::-1] + [kload, gload] + wload + [qload, hload, grload]:
        copy.start()

    barrier = pltpu.get_barrier_semaphore()
    greeted = [z_peer(k) for k in range(1, T)] + [pos_peer(k) for k in range(1, SUB)]
    greeted += [(before, lax.rem(t + k, T)) for k in range(T)]
    greeted += [(after, lax.rem(t + k, T)) for k in range(T)]
    for dev in greeted:
        pl.semaphore_signal(barrier, inc=1, device_id=dev, device_id_type=MESH)
    pl.semaphore_wait(barrier, len(greeted))

    def pass_block(v, p, tt, ssem, kind, dev):
        send(blk(v, p, tt), blk(v, p, tt), ssem, ag_r.at[v, kind, tt], dev)

    def to_pair(v, p, tt):
        pass_block(v, p, tt, ag_s.at[PAIR if p is pos else PAIR_X], FROM_PAIR, pair_dev)

    def ways(*steps):
        for kind, step in steps:
            goal = t + step
            inside = goal >= 0 if step < 0 else goal < T
            yield kind, inside, (sec, lax.min(lax.max(goal, 0), T - 1))

    def own_ways(v=0):
        far, near = ((FAR, -2), (FAR_R, 2)), ((NEAR, -1), (NEAR_R, 1))
        return ways(*(near + far if v == 1 else far + near))

    def near_ways():
        return ways((NEAR_X, -1), (NEAR_XR, 1))

    def along(v):
        for kind, inside, dev in own_ways(v):

            @pl.when(inside)
            def _():
                pass_block(v, pos, t, ag_s.at[kind], FROM_Z, dev)

    def onward_ways(j):
        tt = order[j]
        away = lax.select(tt < t, jnp.int32(1), jnp.int32(-1))
        even = lax.rem((t - tt) * away, 2) == 0
        for step in (1, 2):
            if not any(d % 2 == 0 and d + step < T for d in range((j + 1) // 2, j + 1)):
                continue
            goal = t + step * away
            use = jnp.logical_and(even, jnp.logical_and(goal >= 0, goal < T))
            yield step - 1, use, (sec, lax.min(lax.max(goal, 0), T - 1))

    def is_far(j):
        return jnp.abs(order[j] - t) > 1

    def take(v, j):
        tt = order[j]
        arrived(blk(v, pos, tt), ag_r.at[v, FROM_Z, tt])
        for kind, use, dev in onward_ways(j):

            @pl.when(use)
            def _():
                pass_block(v, pos, tt, relay_s.at[v, j, kind], FROM_Z, dev)

        if v == 1:
            pass_block(v, pos, tt, ag_s.at[ACROSS], FROM_X, x_dev)
        elif j > 1:

            @pl.when(is_far(j))
            def _():
                pass_block(v, pos, tt, far_s.at[j], FROM_X, x_dev)

        to_pair(v, pos, tt)

    def take_x(v, j):
        tt = order[j]
        arrived(blk(v, pos_x, tt), ag_r.at[v, FROM_X, tt])
        if v == 0 and j == 0:
            for kind, inside, dev in near_ways():

                @pl.when(inside)
                def _():
                    pass_block(v, pos_x, tt, ag_s.at[kind], FROM_X, dev)

        to_pair(v, pos_x, tt)

    own[1].wait()
    pass_block(1, pos, t, ag_s.at[ACROSS], FROM_X, x_dev)
    along(1)
    own[0].wait()
    pass_block(0, pos, t, far_s.at[0], FROM_X, x_dev)
    along(0)
    to_pair(1, pos, t)
    to_pair(0, pos, t)
    kload.wait()
    gload.wait()
    for k in range(1, SUB):
        send(kinds.at[pos], kinds.at[pos], small_s.at[0], small_r.at[0], pos_peer(k))
        send(gain_all.at[pos], gain_all.at[pos], small_s.at[1], small_r.at[1], pos_peer(k))

    for copy in wload:
        copy.wait()
    qload.wait()

    def join_weights(v):
        for i in range(T):
            at = pl.ds(i * cols, cols)
            kv_cols = jnp.concatenate([wkv[v, :, at], wvv[v, :, at]], axis=0)
            wcat[v, i, :, hd:] = jnp.transpose(kv_cols)

    def project(v, j):
        tt = order[j]
        arrived(xs.at[0, pl.ds(0, 2)], ag_r.at[v, FROM_PAIR, tt])
        block = tt * cols // gcols
        off = pl.multiple_of(lax.rem(tt * cols, gcols), cols)
        speech = kindc[v, :, 0:1] > 0.5
        pair = gain_all[block, v, :, pl.ds(off, cols)].astype(F32)
        xf = xg[v, tt].astype(F32)
        squares = jnp.broadcast_to(jnp.sum(xf * xf, axis=1, keepdims=True), (n, 128))
        scaled = (xf * jnp.where(speech, pair[1:2, :], pair[0:1, :])).astype(BF16)
        product = dot(scaled, wcat[v, tt], ((1,), (0,)))
        if j == 0:
            square[v] = squares
            acc[v] = product
        else:
            square[v] += squares
            acc[v] += product

    mine = pl.ds(pl.multiple_of(t * kc, kc), kc)
    queries = [None, None]

    def share_keys(v):
        inverse = lax.rsqrt(square[v][:, 0:1] / width + EPS)
        invc[v] = jnp.broadcast_to(inverse, (n, 128))
        projected = acc[v] * inverse
        turned = jnp.transpose(projected[:, hd:]).astype(BF16)
        kvt[v, 0, mine, :] = turned[:kc]
        kvt[v, 1, mine, :] = turned[kc:]
        for k in range(1, T):
            block = kvt.at[v, :, mine, :]
            send(block, block, kv_s.at[v], kv_r.at[v], z_peer(k))
        queries[v] = projected[:, :hd].astype(BF16)

    scale = hd ** (-0.5)
    query_grads = [None, None]

    def attend(v):
        eye = lax.broadcasted_iota(jnp.int32, (n, n), 0) == lax.broadcasted_iota(jnp.int32, (n, n), 1)
        causal = lax.broadcasted_iota(jnp.int32, (n, n), 0) >= lax.broadcasted_iota(
            jnp.int32, (n, n), 1
        )
        arrived(dkv_in.at[:, v], kv_r.at[v])
        kt = kvt[v, 0]
        vt = kvt[v, 1]
        og = hg[v]
        scores = dot(queries[v], kt, ((1,), (0,))) * scale
        scores = jnp.where(causal, scores, -1e30)
        top = jnp.max(scores, axis=1, keepdims=True)
        weights = jnp.exp(scores - top)
        probs = weights / jnp.sum(weights, axis=1, keepdims=True)
        pg = dot(og, vt, ((1,), (0,)))
        sg = probs * (pg - jnp.sum(pg * probs, axis=1, keepdims=True)) * scale
        sg = sg.astype(BF16)
        key_each = dot(queries[v], sg, ((0,), (0,)))
        value_each = dot(og, probs.astype(BF16), ((0,), (0,)))
        dkv[v, 0] = key_each.astype(BF16)
        dkv[v, 1] = value_each.astype(BF16)
        for k in range(1, T):
            goal = pl.ds(pl.multiple_of(lax.rem(t + k, T) * kc, kc), kc)
            send(dkv.at[v, :, goal, :], dkv_in.at[k - 1, v], dk_s.at[v], dk_r.at[v], z_peer(k))
        qg = dot(sg, kt, ((1,), (1,)))
        query_grads[v] = qg.astype(BF16)
        column = jnp.sum(qg * queries[v].astype(F32), axis=1, keepdims=True)
        line = jnp.sum(jnp.where(eye, column, 0.0), axis=0, keepdims=True)
        line = line + jnp.sum(
            key_each * kt.astype(F32) + value_each * vt.astype(F32), axis=0, keepdims=True
        )
        stat[v] = jnp.broadcast_to(line, (8, n))
        for k in range(1, T):
            send(stat.at[v], stat_z.at[v, k - 1], st_s.at[v], st_r.at[v], z_peer(k))

    def share_stat(v):
        line = stat[v]
        arrived(stat_z.at[v], st_r.at[v])
        for k in range(1, T):
            line = line + stat_z[v, k - 1]
        stat_s[v] = line
        for k in range(1, SUB):
            send(stat_s.at[v], stat_in.at[v, k - 1], sp_s.at[v], sp_r.at[v], pos_peer(k))

    def joined_grads(v):
        summed = dkv[v, :, mine, :].astype(F32)
        arrived(dkv_in.at[:, v], dk_r.at[v])
        for k in range(1, T):
            summed = summed + dkv_in[k - 1, v].astype(F32)
        kv_rows = jnp.transpose(summed.reshape(2 * kc, n)).astype(BF16)
        return jnp.concatenate([query_grads[v], kv_rows], axis=1)

    def term(v, joined, j):
        i = order[j]
        piece = dot(joined, wcat[v, i], ((1,), (1,))).astype(BF16)
        for p in range(SUB):
            part[v, i, p % 2, p // 2] = piece[p * rows : (p + 1) * rows]
        send(part.at[v, i, 1 - ci], part_in.at[v, i], pair_s.at[0], pair_r.at[v, i], pair_dev)

    def cross(v, j):
        i = order[j]
        arrived(part_in.at[v, i], pair_r.at[v, i])
        xs[v, i] = (part[v, i, ci, 1 - xi].astype(F32) + part_in[v, i, 1 - xi].astype(F32)).astype(BF16)
        send(xs.at[v, i], xr.at[v, i], x_s.at[0], x_r.at[v, i], x_dev)

    def slot(v, section):
        return lax.select(section == 0, jnp.int32(1 - v), jnp.int32(v))

    def deliver(v, j):
        i = order[j]
        arrived(xr.at[v, i], x_r.at[v, i])
        summed = (
            part[v, i, ci, xi].astype(F32) + part_in[v, i, xi].astype(F32) + xr[v, i].astype(F32)
        )
        inverse = invc[v, rowpos(pos), 0:1]
        speech = kindc[v, rowpos(pos), 0:1] > 0.5
        off = pl.multiple_of(lax.rem(i * cols, gcols), cols)
        pair = gain_all[i * cols // gcols, v, :, pl.ds(off, cols)].astype(F32)
        summed = inverse * jnp.where(speech, pair[1:2, :], pair[0:1, :]) * summed
        if j == 0:
            line = stat_s[v]
            arrived(stat_in.at[v], sp_r.at[v])
            for k in range(1, SUB):
                line = line + stat_in[v, k - 1]
            lane = lax.broadcasted_iota(jnp.int32, (rows, n), 1)
            row = lax.broadcasted_iota(jnp.int32, (rows, n), 0)
            pick = lane == row + pos * rows
            mean = jnp.sum(jnp.where(pick, line[0:1, :], 0.0), axis=1, keepdims=True) / width
            x = xg[v, t, rowpos(pos), :].astype(F32)
            summed = gr[v].astype(F32) + summed - x * (inverse * inverse * mean)
        zs[v, i] = summed.astype(BF16)
        goal = slot(v, here)
        send(zs.at[v, i], zr.at[goal, t], z_s.at[0], z_r.at[goal], (before, i))

    def collect(v):
        goal = slot(v, section_after)
        total = None
        arrived(zr.at[goal], z_r.at[goal])
        for i in range(T):
            theirs = zr[goal, i].astype(F32)
            total = theirs if total is None else total + theirs
        out[goal] = total.astype(BF16)

    def read_kinds():
        eye_r = lax.broadcasted_iota(jnp.int32, (rows, rows), 0) == lax.broadcasted_iota(
            jnp.int32, (rows, rows), 1
        )
        arrived(kinds.at[pl.ds(0, SUB - 1)], small_r.at[0])
        arrived(gain_all.at[pl.ds(0, SUB - 1)], small_r.at[1])
        for v in range(2):
            for p in range(SUB):
                line = kinds[p, v : v + 1, :].astype(F32)
                column = jnp.sum(jnp.where(eye_r, line, 0.0), axis=1, keepdims=True)
                kindc[v, p * rows : (p + 1) * rows, :] = jnp.broadcast_to(column, (rows, 128))

    take(1, 1)
    for j in range(2, T - 1):
        take(1, j)
    take_x(0, 0)
    join_weights(1)
    take(1, T - 1)
    take_x(1, 0)
    read_kinds()
    project(1, 0)
    for j in range(T - 1, 0, -1):
        take(0, j)
    join_weights(0)
    take_x(1, 1)
    for j in range(2, T):
        take_x(1, j)
    for j in range(1, T):
        project(1, j)
    share_keys(1)
    project(0, 0)
    for j in range(T - 1, 0, -1):
        take_x(0, j)
    for j in range(T - 1, 0, -1):
        project(0, j)
    share_keys(0)
    hload.wait()
    grload.wait()
    attend(1)
    attend(0)
    joined = joined_grads(1)
    for j in range(T - 1, -1, -1):
        term(1, joined, j)
        if j < T - 1:
            cross(1, j + 1)
    cross(1, 0)
    share_stat(1)
    joined = joined_grads(0)
    for j in range(T - 1, -1, -1):
        term(0, joined, j)
        if j < T - 1:
            cross(0, j + 1)
            deliver(1, j + 1)
    cross(0, 0)
    share_stat(0)
    deliver(1, 0)
    for j in range(T - 1, -1, -1):
        deliver(0, j)

    for ways_out, size in ((own_ways, part_in.at[0, 0]), (near_ways, xs.at[0, 0])):
        for kind, inside, dev in ways_out():

            @pl.when(inside)
            def _():
                sent(size, ag_s.at[kind])

    sent(xs, ag_s.at[PAIR])
    sent(xs, ag_s.at[PAIR_X])
    sent(xs.at[0], ag_s.at[ACROSS])
    sent(xs.at[0, 0], far_s.at[0])
    for j in range(2, T):

        @pl.when(is_far(j))
        def _():
            sent(xs.at[0, 0], far_s.at[j])

        for v in range(2):
            for kind, use, dev in onward_ways(j):

                @pl.when(use)
                def _():
                    sent(xs.at[0, 0], relay_s.at[v, j, kind])

    sent(kinds.at[pl.ds(0, SUB - 1)], small_s.at[0])
    sent(gain_all.at[pl.ds(0, SUB - 1)], small_s.at[1])
    for v in range(2):
        sent(dkv_in.at[:, v], kv_s.at[v])
        sent(dkv_in.at[:, v], dk_s.at[v])
        sent(stat_z.at[v], st_s.at[v])
    for v in range(2):
        sent(stat_in.at[v], sp_s.at[v])
    sent(part_in, pair_s.at[0])
    sent(xs, x_s.at[0])
    sent(zs, z_s.at[0])
    collect(1)
    collect(0)


def per_device(sections, acts, grads_in, head_grads, types, gains, w_query, w_key, w_value):
    T = lax.axis_size("tensor")
    acts, grads_in, head_grads, types, gains = acts[0], grads_in[0], head_grads[0], types[0], gains[0]
    w_query, w_key, w_value = w_query[0], jnp.swapaxes(w_key[0], 1, 2), jnp.swapaxes(w_value[0], 1, 2)
    spans, rows, cols = acts.shape
    n = SUB * rows
    hd = w_query.shape[2]
    kc = w_key.shape[1]
    w_query = w_query.reshape(spans, T, cols, hd)
    V = pltpu.VMEM
    D = pltpu.SemaphoreType.DMA
    scratch = [
        V((2, T, n, cols), BF16), V((SUB, 2, rows), jnp.int32), V((SUB,) + gains.shape, BF16),
        V(w_key.shape, BF16), V(w_value.shape, BF16),
        V((2, T, cols, hd + 2 * kc), BF16), V(head_grads.shape, BF16), V(grads_in.shape, BF16),
        V((2, n, 128), F32), V((2, n, 128), F32), V((2, n, hd + 2 * kc), F32), V((2, n, 128), F32),
        V((2, 2, hd, n), BF16), V((2, 2, hd, n), BF16), V((T - 1, 2, 2, kc, n), BF16),
        V((2, 8, n), F32), V((2, T - 1, 8, n), F32), V((2, 8, n), F32), V((2, SUB - 1, 8, n), F32),
        V((2, T, 2, 2, rows, cols), BF16), V((2, T, 2, rows, cols), BF16),
        V((2, T, rows, cols), BF16), V((2, T, rows, cols), BF16),
        V((2, T, rows, cols), BF16), V((2, T, rows, cols), BF16),
        D((9,)), D((9,)), D((T,)), D((2, T, 1 if T <= 4 else 2)), D((2, 3, T)), D((2,)), D((2,)),
        D((2,)), D((2,)), D((2,)), D((2,)), D((2,)), D((2,)), D((2,)), D((2,)),
        D((1,)), D((2, T)), D((1,)), D((2, T)), D((1,)), D((2,)),
    ]

    def body(*refs):
        kernel(sections, T, *refs)

    routed = pl.pallas_call(
        body,
        out_shape=jax.ShapeDtypeStruct((2, rows, cols), BF16),
        in_specs=[pl.BlockSpec(memory_space=pl.ANY)] * 8,
        out_specs=pl.BlockSpec(memory_space=pltpu.VMEM),
        scratch_shapes=scratch,
        compiler_params=pltpu.CompilerParams(
            collective_id=0, has_side_effects=True, vmem_limit_bytes=67_000_000
        ),
        name="relay",
    )(acts, grads_in, head_grads, types, gains, w_query, w_key, w_value)
    return routed[None]


def solution(mesh):
    sections = mesh.shape["section"] // SUB

    def run(*args):
        return per_device(sections, *args)

    return jax.shard_map(
        run,
        mesh=mesh,
        in_specs=(
            P("section", None, None, "tensor"),
            P("section", None, None, "tensor"),
            P("section", None, None, "tensor"),
            P("section", None, None),
            P("section", None, None, None),
            P("section", None, None, "tensor"),
            P("section", None, None, "tensor"),
            P("section", None, None, "tensor"),
        ),
        out_specs=P("section", None, None, "tensor"),
        check_vma=False,
    )
```

```python
import jax
import jax.numpy as jnp
from jax import lax
from jax.experimental import pallas as pl
from jax.experimental.pallas import tpu as pltpu
from jax.sharding import PartitionSpec as P

SUB = 4
EPS = 1e-05
MESH = pl.DeviceIdType.MESH
F32 = jnp.float32
BF16 = jnp.bfloat16
ACROSS, PAIR, PAIR_X = 0, 2, 3
FROM_Z, FROM_X, FROM_PAIR = range(3)


def dot(a, b, dims):
    return lax.dot_general(a, b, (dims, ((), ())), preferred_element_type=F32)


def kernel(
    sections, tensors,
    acts, grads, heads, types, gains, wq, wk, wv,
    out,
    xg, kinds, gain_all, wkv, wvv, wcat, hg, gr, kindc, invc, acc, square,
    kvt, dkv, dkv_in, stat, stat_z, stat_s, stat_in,
    part, part_in, xs, xr, zs,
    loc, ag_s, own_s, near_s, far_s, relay_s, ag_r, small_s, small_r, kv_s, kv_r, dk_s, dk_r, st_s, st_r, sp_s, sp_r,
    pair_s, pair_r, x_s, x_r, z_s, z_r,
):
    spans, rows, cols = acts.shape
    n = SUB * rows
    hd = wq.shape[3]
    kc = wk.shape[1]
    width = cols * tensors
    gcols = gains.shape[2]
    T = tensors
    t = lax.axis_index("tensor")
    sec = lax.axis_index("section")
    pos = lax.rem(sec, SUB)
    here = sec // SUB
    base = here * SUB
    xi = pos // 2
    ci = lax.rem(pos, 2)
    pos_pair = xi * 2 + (1 - ci)
    pos_x = (1 - xi) * 2 + ci
    pos_diag = (1 - xi) * 2 + (1 - ci)
    pair_dev = (base + pos_pair, t)
    x_dev = (base + pos_x, t)
    section_before = lax.rem(here + sections - 1, sections)
    section_after = lax.rem(here + 1, sections)
    before = section_before * SUB + pos
    after = section_after * SUB + pos

    both = 2 * lax.min(t, T - 1 - t)
    order = [t]
    for j in range(1, T):
        d = (j + 1) // 2
        near = t - d if j % 2 else t + d
        rest = lax.select(2 * t < T - 1, jnp.int32(j), jnp.int32(T - 1 - j))
        order.append(lax.select(j <= both, near, rest))

    def pos_peer(k):
        return (base + lax.rem(pos + k, SUB), t)

    def z_peer(k):
        return (sec, lax.rem(t + k, T))

    def send(src, dst, ssem, rsem, dev):
        pltpu.make_async_remote_copy(
            src_ref=src, dst_ref=dst, send_sem=ssem, recv_sem=rsem, device_id=dev, device_id_type=MESH
        ).start()

    def sent(src, ssem):
        pltpu.make_async_copy(src, src, ssem).wait()

    def arrived(dst, rsem):
        pltpu.make_async_copy(dst, dst, rsem).wait()

    def rowpos(p):
        return pl.ds(pl.multiple_of(p * rows, rows), rows)

    def blk(v, p, tt):
        return xg.at[v, tt, rowpos(p), :]

    own = [pltpu.make_async_copy(acts.at[v], blk(v, pos, t), loc.at[v]) for v in range(2)]
    kload = pltpu.make_async_copy(types, kinds.at[pos], loc.at[2])
    gload = pltpu.make_async_copy(gains, gain_all.at[pos], loc.at[3])
    wload = [
        pltpu.make_async_copy(wk, wkv, loc.at[5]),
        pltpu.make_async_copy(wv, wvv, loc.at[6]),
    ]
    qload = pltpu.make_async_copy(wq, wcat.at[:, :, :, pl.ds(0, hd)], loc.at[4])
    hload = pltpu.make_async_copy(heads, hg, loc.at[7])
    grload = pltpu.make_async_copy(grads, gr, loc.at[8])
    for copy in own[::-1] + [kload, gload] + wload + [qload, hload, grload]:
        copy.start()

    barrier = pltpu.get_barrier_semaphore()
    greeted = [z_peer(k) for k in range(1, T)] + [pos_peer(k) for k in range(1, SUB)]
    greeted += [(before, lax.rem(t + k, T)) for k in range(T)]
    if sections > 2:
        greeted += [(after, lax.rem(t + k, T)) for k in range(T)]
    for dev in greeted:
        pl.semaphore_signal(barrier, inc=1, device_id=dev, device_id_type=MESH)
    pl.semaphore_wait(barrier, len(greeted))

    across_all = (1,)
    reach, nearest_first = (2, 2), (False, True)

    def pass_block(v, p, tt, ssem, kind, dev):
        send(blk(v, p, tt), blk(v, p, tt), ssem, ag_r.at[v, kind, tt], dev)

    def to_pair(v, p, tt):
        pass_block(v, p, tt, ag_s.at[PAIR if p is pos else PAIR_X], FROM_PAIR, pair_dev)

    def ways(*steps):
        for kind, step in steps:
            goal = t + step
            inside = goal >= 0 if step < 0 else goal < T
            yield kind, inside, (sec, lax.min(lax.max(goal, 0), T - 1))

    def own_ways(v):
        steps = range(1, reach[v] + 1)
        steps = steps if nearest_first[v] else steps[::-1]
        return ways(*((own_s.at[v, d - 1, side], (d, -d)[side]) for d in steps for side in range(2)))

    def near_ways(v):
        return ways((near_s.at[v, 0], -1), (near_s.at[v, 1], 1))

    def along(v):
        for ssem, inside, dev in own_ways(v):

            @pl.when(inside)
            def _():
                pass_block(v, pos, t, ssem, FROM_Z, dev)

    def onward_ways(v, j):
        tt, most = order[j], reach[v]
        away = lax.select(tt < t, jnp.int32(1), jnp.int32(-1))
        turn = lax.rem((t - tt) * away, most) == 0
        for step in range(1, most + 1):
            if not any(d % most == 0 and d + step < T for d in range((j + 1) // 2, j + 1)):
                continue
            goal = t + step * away
            use = jnp.logical_and(turn, jnp.logical_and(goal >= 0, goal < T))
            yield relay_s.at[v, j, step - 1], use, (sec, lax.min(lax.max(goal, 0), T - 1))

    def is_far(j):
        return jnp.abs(order[j] - t) > 1

    def take(v, j):
        tt = order[j]
        arrived(blk(v, pos, tt), ag_r.at[v, FROM_Z, tt])
        for ssem, use, dev in onward_ways(v, j):

            @pl.when(use)
            def _():
                pass_block(v, pos, tt, ssem, FROM_Z, dev)

        if v in across_all:
            pass_block(v, pos, tt, ag_s.at[ACROSS + v], FROM_X, x_dev)
        elif j > 1:

            @pl.when(is_far(j))
            def _():
                pass_block(v, pos, tt, far_s.at[v, j], FROM_X, x_dev)

        to_pair(v, pos, tt)

    def take_direct(v, j, direct):
        @pl.when((jnp.abs(order[j] - t) <= reach[v]) == direct)
        def _():
            take(v, j)

    def take_x(v, j):
        tt = order[j]
        arrived(blk(v, pos_x, tt), ag_r.at[v, FROM_X, tt])
        if v not in across_all and j == 0:
            for ssem, inside, dev in near_ways(v):

                @pl.when(inside)
                def _():
                    pass_block(v, pos_x, tt, ssem, FROM_X, dev)

        to_pair(v, pos_x, tt)

    def across(v):
        pass_block(v, pos, t, ag_s.at[ACROSS + v] if v in across_all else far_s.at[v, 0], FROM_X, x_dev)

    own[1].wait()
    across(1)
    along(1)
    own[0].wait()
    across(0)
    along(0)
    to_pair(1, pos, t)
    to_pair(0, pos, t)
    kload.wait()
    gload.wait()
    for k in range(1, SUB):
        send(kinds.at[pos], kinds.at[pos], small_s.at[0], small_r.at[0], pos_peer(k))
        send(gain_all.at[pos], gain_all.at[pos], small_s.at[1], small_r.at[1], pos_peer(k))

    for copy in wload:
        copy.wait()
    qload.wait()

    def join_weights(v):
        for i in range(T):
            at = pl.ds(i * cols, cols)
            kv_cols = jnp.concatenate([wkv[v, :, at], wvv[v, :, at]], axis=0)
            wcat[v, i, :, hd:] = jnp.transpose(kv_cols)

    def project(v, j):
        tt = order[j]
        arrived(xs.at[0, pl.ds(0, 2)], ag_r.at[v, FROM_PAIR, tt])
        block = tt * cols // gcols
        off = pl.multiple_of(lax.rem(tt * cols, gcols), cols)
        speech = kindc[v, :, 0:1] > 0.5
        pair = gain_all[block, v, :, pl.ds(off, cols)].astype(F32)
        xf = xg[v, tt].astype(F32)
        squares = jnp.broadcast_to(jnp.sum(xf * xf, axis=1, keepdims=True), (n, 128))
        scaled = (xf * jnp.where(speech, pair[1:2, :], pair[0:1, :])).astype(BF16)
        product = dot(scaled, wcat[v, tt], ((1,), (0,)))
        if j == 0:
            square[v] = squares
            acc[v] = product
        else:
            square[v] += squares
            acc[v] += product

    mine = pl.ds(pl.multiple_of(t * kc, kc), kc)
    queries = [None, None]

    def share_keys(v):
        inverse = lax.rsqrt(square[v][:, 0:1] / width + EPS)
        invc[v] = jnp.broadcast_to(inverse, (n, 128))
        projected = acc[v] * inverse
        turned = jnp.transpose(projected[:, hd:]).astype(BF16)
        kvt[v, 0, mine, :] = turned[:kc]
        kvt[v, 1, mine, :] = turned[kc:]
        for k in range(1, T):
            block = kvt.at[v, :, mine, :]
            send(block, block, kv_s.at[v], kv_r.at[v], z_peer(k))
        queries[v] = projected[:, :hd].astype(BF16)

    scale = hd ** (-0.5)
    query_grads = [None, None]

    def attend(v):
        eye = lax.broadcasted_iota(jnp.int32, (n, n), 0) == lax.broadcasted_iota(jnp.int32, (n, n), 1)
        causal = lax.broadcasted_iota(jnp.int32, (n, n), 0) >= lax.broadcasted_iota(
            jnp.int32, (n, n), 1
        )
        arrived(dkv_in.at[:, v], kv_r.at[v])
        kt = kvt[v, 0]
        vt = kvt[v, 1]
        og = hg[v]
        scores = dot(queries[v], kt, ((1,), (0,))) * scale
        scores = jnp.where(causal, scores, -1e30)
        top = jnp.max(scores, axis=1, keepdims=True)
        weights = jnp.exp(scores - top)
        probs = weights / jnp.sum(weights, axis=1, keepdims=True)
        pg = dot(og, vt, ((1,), (0,)))
        sg = probs * (pg - jnp.sum(pg * probs, axis=1, keepdims=True)) * scale
        sg = sg.astype(BF16)
        key_each = dot(queries[v], sg, ((0,), (0,)))
        value_each = dot(og, probs.astype(BF16), ((0,), (0,)))
        dkv[v, 0] = key_each.astype(BF16)
        dkv[v, 1] = value_each.astype(BF16)
        for k in range(1, T):
            goal = pl.ds(pl.multiple_of(lax.rem(t + k, T) * kc, kc), kc)
            send(dkv.at[v, :, goal, :], dkv_in.at[k - 1, v], dk_s.at[v], dk_r.at[v], z_peer(k))
        qg = dot(sg, kt, ((1,), (1,)))
        query_grads[v] = qg.astype(BF16)
        column = jnp.sum(qg * queries[v].astype(F32), axis=1, keepdims=True)
        line = jnp.sum(jnp.where(eye, column, 0.0), axis=0, keepdims=True)
        line = line + jnp.sum(
            key_each * kt.astype(F32) + value_each * vt.astype(F32), axis=0, keepdims=True
        )
        stat[v] = jnp.broadcast_to(line, (8, n))
        for k in range(1, T):
            send(stat.at[v], stat_z.at[v, k - 1], st_s.at[v], st_r.at[v], z_peer(k))

    def share_stat(v):
        line = stat[v]
        arrived(stat_z.at[v], st_r.at[v])
        for k in range(1, T):
            line = line + stat_z[v, k - 1]
        stat_s[v] = line
        for k in range(1, SUB):
            send(stat_s.at[v], stat_in.at[v, k - 1], sp_s.at[v], sp_r.at[v], pos_peer(k))

    def joined_grads(v):
        summed = dkv[v, :, mine, :].astype(F32)
        arrived(dkv_in.at[:, v], dk_r.at[v])
        for k in range(1, T):
            summed = summed + dkv_in[k - 1, v].astype(F32)
        kv_rows = jnp.transpose(summed.reshape(2 * kc, n)).astype(BF16)
        return jnp.concatenate([query_grads[v], kv_rows], axis=1)

    def term(v, joined, j):
        i = order[j]
        piece = dot(joined, wcat[v, i], ((1,), (1,))).astype(BF16)
        for p in range(SUB):
            part[v, i, p % 2, p // 2] = piece[p * rows : (p + 1) * rows]
        for x in (1 - xi, xi):
            kind = lax.rem(x + xi, 2)
            send(part.at[v, i, 1 - ci, x], part_in.at[v, i, x], pair_s.at[0], pair_r.at[v, kind, i], pair_dev)

    def cross(v, j):
        i = order[j]
        arrived(part_in.at[v, i, 1 - xi], pair_r.at[v, 1, i])
        xs[v, i] = (part[v, i, ci, 1 - xi].astype(F32) + part_in[v, i, 1 - xi].astype(F32)).astype(BF16)
        send(xs.at[v, i], xr.at[v, i], x_s.at[0], x_r.at[v, i], x_dev)

    def slot(v, section):
        return lax.select(section == 0, jnp.int32(1 - v), jnp.int32(v))

    def deliver(v, j):
        i = order[j]
        arrived(part_in.at[v, i, xi], pair_r.at[v, 0, i])
        arrived(xr.at[v, i], x_r.at[v, i])
        summed = (
            part[v, i, ci, xi].astype(F32) + part_in[v, i, xi].astype(F32) + xr[v, i].astype(F32)
        )
        inverse = invc[v, rowpos(pos), 0:1]
        speech = kindc[v, rowpos(pos), 0:1] > 0.5
        off = pl.multiple_of(lax.rem(i * cols, gcols), cols)
        pair = gain_all[i * cols // gcols, v, :, pl.ds(off, cols)].astype(F32)
        summed = inverse * jnp.where(speech, pair[1:2, :], pair[0:1, :]) * summed
        if j == 0:
            line = stat_s[v]
            arrived(stat_in.at[v], sp_r.at[v])
            for k in range(1, SUB):
                line = line + stat_in[v, k - 1]
            lane = lax.broadcasted_iota(jnp.int32, (rows, n), 1)
            row = lax.broadcasted_iota(jnp.int32, (rows, n), 0)
            pick = lane == row + pos * rows
            mean = jnp.sum(jnp.where(pick, line[0:1, :], 0.0), axis=1, keepdims=True) / width
            x = xg[v, t, rowpos(pos), :].astype(F32)
            summed = gr[v].astype(F32) + summed - x * (inverse * inverse * mean)
        zs[v, i] = summed.astype(BF16)
        goal = slot(v, here)
        send(zs.at[v, i], out.at[goal, t], z_s.at[0], z_r.at[goal], (before, i))

    def collect(v):
        goal = slot(v, section_after)
        arrived(out.at[goal], z_r.at[goal])

    def read_kinds():
        eye_r = lax.broadcasted_iota(jnp.int32, (rows, rows), 0) == lax.broadcasted_iota(
            jnp.int32, (rows, rows), 1
        )
        arrived(kinds.at[pl.ds(0, SUB - 1)], small_r.at[0])
        arrived(gain_all.at[pl.ds(0, SUB - 1)], small_r.at[1])
        for v in range(2):
            for p in range(SUB):
                line = kinds[p, v : v + 1, :].astype(F32)
                column = jnp.sum(jnp.where(eye_r, line, 0.0), axis=1, keepdims=True)
                kindc[v, p * rows : (p + 1) * rows, :] = jnp.broadcast_to(column, (rows, 128))

    take(1, 1)
    for j in range(2, T - 1):
        take(1, j)
    join_weights(1)
    take(1, T - 1)
    take_x(1, 0)
    take_x(0, 0)
    read_kinds()
    project(1, 0)
    for j in range(T - 1, 0, -1):
        take(0, j)
    join_weights(0)
    take_x(1, 1)
    for j in range(2, T):
        take_x(1, j)
    for j in range(1, T):
        project(1, j)
    share_keys(1)
    project(0, 0)
    take_x(0, 3)
    take_x(0, 2)
    project(0, 3)
    take_x(0, 1)
    project(0, 2)
    project(0, 1)
    share_keys(0)
    hload.wait()
    grload.wait()
    attend(1)
    attend(0)
    joined = joined_grads(1)
    for j in range(T - 1, -1, -1):
        term(1, joined, j)
        if j < T - 1:
            cross(1, j + 1)
    cross(1, 0)
    share_stat(1)
    joined = joined_grads(0)
    for j in range(T - 1, -1, -1):
        term(0, joined, j)
        if j < T - 1:
            cross(0, j + 1)
            deliver(1, j + 1)
    cross(0, 0)
    share_stat(0)
    deliver(1, 0)
    for j in range(T - 1, -1, -1):
        deliver(0, j)

    for v in range(2):
        for ssem, inside, dev in own_ways(v):

            @pl.when(inside)
            def _():
                sent(xs.at[0, 0], ssem)

        if v in across_all:
            sent(xs.at[0], ag_s.at[ACROSS + v])
        else:
            sent(xs.at[0, 0], far_s.at[v, 0])
            for ssem, inside, dev in near_ways(v):

                @pl.when(inside)
                def _():
                    sent(xs.at[0, 0], ssem)

        for j in range(1, T):
            for ssem, use, dev in onward_ways(v, j):

                @pl.when(use)
                def _():
                    sent(xs.at[0, 0], ssem)

            if v not in across_all and j > 1:

                @pl.when(is_far(j))
                def _():
                    sent(xs.at[0, 0], far_s.at[v, j])

    sent(xs, ag_s.at[PAIR])
    sent(xs, ag_s.at[PAIR_X])
    sent(kinds.at[pl.ds(0, SUB - 1)], small_s.at[0])
    sent(gain_all.at[pl.ds(0, SUB - 1)], small_s.at[1])
    for v in range(2):
        sent(dkv_in.at[:, v], kv_s.at[v])
        sent(dkv_in.at[:, v], dk_s.at[v])
        sent(stat_z.at[v], st_s.at[v])
    for v in range(2):
        sent(stat_in.at[v], sp_s.at[v])
    sent(part_in, pair_s.at[0])
    sent(xs, x_s.at[0])
    sent(zs, z_s.at[0])
    collect(1)
    collect(0)


def per_device(sections, acts, grads_in, head_grads, types, gains, w_query, w_key, w_value):
    T = lax.axis_size("tensor")
    acts, grads_in, head_grads, types, gains = acts[0], grads_in[0], head_grads[0], types[0], gains[0]
    w_query, w_key, w_value = w_query[0], jnp.swapaxes(w_key[0], 1, 2), jnp.swapaxes(w_value[0], 1, 2)
    spans, rows, cols = acts.shape
    n = SUB * rows
    hd = w_query.shape[2]
    kc = w_key.shape[1]
    w_query = w_query.reshape(spans, T, cols, hd)
    V = pltpu.VMEM
    D = pltpu.SemaphoreType.DMA
    scratch = [
        V((2, T, n, cols), BF16), V((SUB, 2, rows), jnp.int32), V((SUB,) + gains.shape, BF16),
        V(w_key.shape, BF16), V(w_value.shape, BF16),
        V((2, T, cols, hd + 2 * kc), BF16), V(head_grads.shape, BF16), V(grads_in.shape, BF16),
        V((2, n, 128), F32), V((2, n, 128), F32), V((2, n, hd + 2 * kc), F32), V((2, n, 128), F32),
        V((2, 2, hd, n), BF16), V((2, 2, hd, n), BF16), V((T - 1, 2, 2, kc, n), BF16),
        V((2, 8, n), F32), V((2, T - 1, 8, n), F32), V((2, 8, n), F32), V((2, SUB - 1, 8, n), F32),
        V((2, T, 2, 2, rows, cols), BF16), V((2, T, 2, rows, cols), BF16),
        V((2, T, rows, cols), BF16), V((2, T, rows, cols), BF16), V((2, T, rows, cols), BF16),
        D((9,)), D((4,)), D((2, 3, 2)), D((2, 2)), D((2, T)), D((2, T, 1 if T <= 4 else 3)), D((2, 3, T)), D((2,)), D((2,)),
        D((2,)), D((2,)), D((2,)), D((2,)), D((2,)), D((2,)), D((2,)), D((2,)),
        D((1,)), D((2, 2, T)), D((1,)), D((2, T)), D((1,)), D((2,)),
    ]

    def body(*refs):
        kernel(sections, T, *refs)

    routed = pl.pallas_call(
        body,
        out_shape=jax.ShapeDtypeStruct((2, T, rows, cols), BF16),
        in_specs=[pl.BlockSpec(memory_space=pl.ANY)] * 8,
        out_specs=pl.BlockSpec(memory_space=pl.ANY),
        scratch_shapes=scratch,
        compiler_params=pltpu.CompilerParams(
            collective_id=0, has_side_effects=True, vmem_limit_bytes=67_000_000
        ),
        name="relay",
    )(acts, grads_in, head_grads, types, gains, w_query, w_key, w_value)
    return jnp.sum(routed.astype(F32), axis=1).astype(BF16)[None]


def solution(mesh):
    sections = mesh.shape["section"] // SUB

    def run(*args):
        return per_device(sections, *args)

    return jax.shard_map(
        run,
        mesh=mesh,
        in_specs=(
            P("section", None, None, "tensor"),
            P("section", None, None, "tensor"),
            P("section", None, None, "tensor"),
            P("section", None, None),
            P("section", None, None, None),
            P("section", None, None, "tensor"),
            P("section", None, None, "tensor"),
            P("section", None, None, "tensor"),
        ),
        out_specs=P("section", None, None, "tensor"),
        check_vma=False,
    )
```

```python
import jax
import jax.numpy as jnp
from jax import lax
from jax.experimental import pallas as pl
from jax.experimental.pallas import tpu as pltpu
from jax.sharding import PartitionSpec as P

SUB = 4
EPS = 1e-05
MESH = pl.DeviceIdType.MESH
F32 = jnp.float32
BF16 = jnp.bfloat16
ACROSS, PAIR, PAIR_X = 0, 2, 3
FROM_Z, FROM_X, FROM_PAIR = range(3)


def dot(a, b, dims):
    return lax.dot_general(a, b, (dims, ((), ())), preferred_element_type=F32)


def kernel(
    sections, tensors,
    acts, grads, heads, types, gains, wq, wk, wv,
    out,
    xg, kinds, gain_all, wkv, wvv, wcat, hg, gr, kindc, invc, acc, square,
    kvt, dkv, dkv_in, stat, stat_z, stat_s, stat_in,
    part, part_in, xs, xr, zs,
    loc, ag_s, own_s, near_s, far_s, relay_s, ag_r, small_s, small_r, kv_s, kv_r, dk_s, dk_r, st_s, st_r, sp_s, sp_r,
    pair_s, pair_r, x_s, x_r, z_s, z_r,
):
    spans, rows, cols = acts.shape
    n = SUB * rows
    hd = wq.shape[3]
    kc = wk.shape[1]
    width = cols * tensors
    gcols = gains.shape[2]
    T = tensors
    t = lax.axis_index("tensor")
    sec = lax.axis_index("section")
    pos = lax.rem(sec, SUB)
    here = sec // SUB
    base = here * SUB
    xi = pos // 2
    ci = lax.rem(pos, 2)
    pos_pair = xi * 2 + (1 - ci)
    pos_x = (1 - xi) * 2 + ci
    pos_diag = (1 - xi) * 2 + (1 - ci)
    pair_dev = (base + pos_pair, t)
    x_dev = (base + pos_x, t)
    section_before = lax.rem(here + sections - 1, sections)
    section_after = lax.rem(here + 1, sections)
    before = section_before * SUB + pos
    after = section_after * SUB + pos

    both = 2 * lax.min(t, T - 1 - t)
    order = [t]
    for j in range(1, T):
        d = (j + 1) // 2
        near = t - d if j % 2 else t + d
        rest = lax.select(2 * t < T - 1, jnp.int32(j), jnp.int32(T - 1 - j))
        order.append(lax.select(j <= both, near, rest))

    def pos_peer(k):
        return (base + lax.rem(pos + k, SUB), t)

    def z_peer(k):
        return (sec, lax.rem(t + k, T))

    def send(src, dst, ssem, rsem, dev):
        pltpu.make_async_remote_copy(
            src_ref=src, dst_ref=dst, send_sem=ssem, recv_sem=rsem, device_id=dev, device_id_type=MESH
        ).start()

    def sent(src, ssem):
        pltpu.make_async_copy(src, src, ssem).wait()

    def arrived(dst, rsem):
        pltpu.make_async_copy(dst, dst, rsem).wait()

    def rowpos(p):
        return pl.ds(pl.multiple_of(p * rows, rows), rows)

    def blk(v, p, tt):
        return xg.at[v, tt, rowpos(p), :]

    own = [pltpu.make_async_copy(acts.at[v], blk(v, pos, t), loc.at[v]) for v in range(2)]
    kload = pltpu.make_async_copy(types, kinds.at[pos], loc.at[2])
    gload = pltpu.make_async_copy(gains, gain_all.at[pos], loc.at[3])
    wload = [
        pltpu.make_async_copy(wk, wkv, loc.at[5]),
        pltpu.make_async_copy(wv, wvv, loc.at[6]),
    ]
    qload = pltpu.make_async_copy(wq, wcat.at[:, :, :, pl.ds(0, hd)], loc.at[4])
    hload = pltpu.make_async_copy(heads, hg, loc.at[7])
    grload = pltpu.make_async_copy(grads, gr, loc.at[8])
    for copy in own[::-1] + [kload, gload] + wload + [qload, hload, grload]:
        copy.start()

    barrier = pltpu.get_barrier_semaphore()
    greeted = [z_peer(k) for k in range(1, T)] + [pos_peer(k) for k in range(1, SUB)]
    greeted += [(before, lax.rem(t + k, T)) for k in range(T)]
    if sections > 2:
        greeted += [(after, lax.rem(t + k, T)) for k in range(T)]
    for dev in greeted:
        pl.semaphore_signal(barrier, inc=1, device_id=dev, device_id_type=MESH)
    pl.semaphore_wait(barrier, len(greeted))

    across_all = (1,)
    reach, nearest_first = (2, 2), (False, True)

    def pass_block(v, p, tt, ssem, kind, dev):
        send(blk(v, p, tt), blk(v, p, tt), ssem, ag_r.at[v, kind, tt], dev)

    def to_pair(v, p, tt):
        pass_block(v, p, tt, ag_s.at[PAIR if p is pos else PAIR_X], FROM_PAIR, pair_dev)

    def ways(*steps):
        for kind, step in steps:
            goal = t + step
            inside = goal >= 0 if step < 0 else goal < T
            yield kind, inside, (sec, lax.min(lax.max(goal, 0), T - 1))

    def own_ways(v):
        steps = range(1, reach[v] + 1)
        steps = steps if nearest_first[v] else steps[::-1]
        return ways(*((own_s.at[v, d - 1, side], (d, -d)[side]) for d in steps for side in range(2)))

    def near_ways(v):
        return ways((near_s.at[v, 0], -1), (near_s.at[v, 1], 1))

    def along(v):
        for ssem, inside, dev in own_ways(v):

            @pl.when(inside)
            def _():
                pass_block(v, pos, t, ssem, FROM_Z, dev)

    def onward_ways(v, j):
        tt, most = order[j], reach[v]
        away = lax.select(tt < t, jnp.int32(1), jnp.int32(-1))
        turn = lax.rem((t - tt) * away, most) == 0
        for step in range(1, most + 1):
            if not any(d % most == 0 and d + step < T for d in range((j + 1) // 2, j + 1)):
                continue
            goal = t + step * away
            use = jnp.logical_and(turn, jnp.logical_and(goal >= 0, goal < T))
            yield relay_s.at[v, j, step - 1], use, (sec, lax.min(lax.max(goal, 0), T - 1))

    def is_far(j):
        return jnp.abs(order[j] - t) > 1

    def take(v, j):
        tt = order[j]
        arrived(blk(v, pos, tt), ag_r.at[v, FROM_Z, tt])
        for ssem, use, dev in onward_ways(v, j):

            @pl.when(use)
            def _():
                pass_block(v, pos, tt, ssem, FROM_Z, dev)

        if v in across_all:
            pass_block(v, pos, tt, ag_s.at[ACROSS + v], FROM_X, x_dev)
        elif j > 1:

            @pl.when(is_far(j))
            def _():
                pass_block(v, pos, tt, far_s.at[v, j], FROM_X, x_dev)

        to_pair(v, pos, tt)

    def take_x(v, j):
        tt = order[j]
        arrived(blk(v, pos_x, tt), ag_r.at[v, FROM_X, tt])
        if v not in across_all and j == 0:
            for ssem, inside, dev in near_ways(v):

                @pl.when(inside)
                def _():
                    pass_block(v, pos_x, tt, ssem, FROM_X, dev)

        to_pair(v, pos_x, tt)

    def across(v):
        pass_block(v, pos, t, ag_s.at[ACROSS + v] if v in across_all else far_s.at[v, 0], FROM_X, x_dev)

    own[1].wait()
    across(1)
    along(1)
    own[0].wait()
    across(0)
    along(0)
    to_pair(1, pos, t)
    to_pair(0, pos, t)
    kload.wait()
    gload.wait()
    for k in range(1, SUB):
        send(kinds.at[pos], kinds.at[pos], small_s.at[0], small_r.at[0], pos_peer(k))
        send(gain_all.at[pos], gain_all.at[pos], small_s.at[1], small_r.at[1], pos_peer(k))

    for copy in wload:
        copy.wait()
    qload.wait()

    def join_weights(v):
        for i in range(T):
            at = pl.ds(i * cols, cols)
            kv_cols = jnp.concatenate([wkv[v, :, at], wvv[v, :, at]], axis=0)
            wcat[v, i, :, hd:] = jnp.transpose(kv_cols)

    def project(v, *blocks):
        for j in blocks:
            arrived(xs.at[0, pl.ds(0, 2)], ag_r.at[v, FROM_PAIR, order[j]])
        speech = kindc[v, :, 0:1] > 0.5
        squares, product = None, None
        for j in blocks:
            tt = order[j]
            block = tt * cols // gcols
            off = pl.multiple_of(lax.rem(tt * cols, gcols), cols)
            pair = gain_all[block, v, :, pl.ds(off, cols)].astype(F32)
            xf = xg[v, tt].astype(F32)
            square_j = jnp.sum(xf * xf, axis=1, keepdims=True)
            scaled = (xf * jnp.where(speech, pair[1:2, :], pair[0:1, :])).astype(BF16)
            product_j = dot(scaled, wcat[v, tt], ((1,), (0,)))
            squares = square_j if squares is None else squares + square_j
            product = product_j if product is None else product + product_j
        squares = jnp.broadcast_to(squares, (n, 128))
        if 0 in blocks:
            square[v] = squares
            acc[v] = product
        else:
            square[v] += squares
            acc[v] += product

    mine = pl.ds(pl.multiple_of(t * kc, kc), kc)
    queries = [None, None]

    def share_keys(v):
        inverse = lax.rsqrt(square[v][:, 0:1] / width + EPS)
        invc[v] = jnp.broadcast_to(inverse, (n, 128))
        projected = acc[v] * inverse
        turned = jnp.transpose(projected[:, hd:]).astype(BF16)
        kvt[v, 0, mine, :] = turned[:kc]
        kvt[v, 1, mine, :] = turned[kc:]
        for k in range(1, T):
            block = kvt.at[v, :, mine, :]
            send(block, block, kv_s.at[v], kv_r.at[v], z_peer(k))
        queries[v] = projected[:, :hd].astype(BF16)

    scale = hd ** (-0.5)
    query_grads = [None, None]

    def attend(v):
        eye = lax.broadcasted_iota(jnp.int32, (n, n), 0) == lax.broadcasted_iota(jnp.int32, (n, n), 1)
        causal = lax.broadcasted_iota(jnp.int32, (n, n), 0) >= lax.broadcasted_iota(
            jnp.int32, (n, n), 1
        )
        arrived(dkv_in.at[:, v], kv_r.at[v])
        kt = kvt[v, 0]
        vt = kvt[v, 1]
        og = hg[v]
        scores = dot(queries[v], kt, ((1,), (0,))) * scale
        scores = jnp.where(causal, scores, -1e30)
        top = jnp.max(scores, axis=1, keepdims=True)
        weights = jnp.exp(scores - top)
        probs = weights / jnp.sum(weights, axis=1, keepdims=True)
        pg = dot(og, vt, ((1,), (0,)))
        sg = probs * (pg - jnp.sum(pg * probs, axis=1, keepdims=True)) * scale
        sg = sg.astype(BF16)
        key_each = dot(queries[v], sg, ((0,), (0,)))
        value_each = dot(og, probs.astype(BF16), ((0,), (0,)))
        dkv[v, 0] = key_each.astype(BF16)
        dkv[v, 1] = value_each.astype(BF16)
        for k in range(1, T):
            goal = pl.ds(pl.multiple_of(lax.rem(t + k, T) * kc, kc), kc)
            send(dkv.at[v, :, goal, :], dkv_in.at[k - 1, v], dk_s.at[v], dk_r.at[v], z_peer(k))
        qg = dot(sg, kt, ((1,), (1,)))
        query_grads[v] = qg.astype(BF16)
        column = jnp.sum(qg * queries[v].astype(F32), axis=1, keepdims=True)
        line = jnp.sum(jnp.where(eye, column, 0.0), axis=0, keepdims=True)
        line = line + jnp.sum(
            key_each * kt.astype(F32) + value_each * vt.astype(F32), axis=0, keepdims=True
        )
        stat[v] = jnp.broadcast_to(line, (8, n))
        for k in range(1, T):
            send(stat.at[v], stat_z.at[v, k - 1], st_s.at[v], st_r.at[v], z_peer(k))

    def share_stat(v):
        line = stat[v]
        arrived(stat_z.at[v], st_r.at[v])
        for k in range(1, T):
            line = line + stat_z[v, k - 1]
        stat_s[v] = line
        for k in range(1, SUB):
            send(stat_s.at[v], stat_in.at[v, k - 1], sp_s.at[v], sp_r.at[v], pos_peer(k))

    def joined_grads(v):
        summed = dkv[v, :, mine, :].astype(F32)
        arrived(dkv_in.at[:, v], dk_r.at[v])
        for k in range(1, T):
            summed = summed + dkv_in[k - 1, v].astype(F32)
        kv_rows = jnp.transpose(summed.reshape(2 * kc, n)).astype(BF16)
        return jnp.concatenate([query_grads[v], kv_rows], axis=1)

    def term(v, joined, j):
        i = order[j]
        piece = dot(joined, wcat[v, i], ((1,), (1,))).astype(BF16)
        for p in range(SUB):
            part[v, i, p % 2, p // 2] = piece[p * rows : (p + 1) * rows]
        for x in (1 - xi, xi):
            kind = lax.rem(x + xi, 2)
            send(part.at[v, i, 1 - ci, x], part_in.at[v, i, x], pair_s.at[0], pair_r.at[v, kind, i], pair_dev)

    def cross(v, j):
        i = order[j]
        arrived(part_in.at[v, i, 1 - xi], pair_r.at[v, 1, i])
        xs[v, i] = (part[v, i, ci, 1 - xi].astype(F32) + part_in[v, i, 1 - xi].astype(F32)).astype(BF16)
        send(xs.at[v, i], xr.at[v, i], x_s.at[0], x_r.at[v, i], x_dev)

    def slot(v, section):
        return lax.select(section == 0, jnp.int32(1 - v), jnp.int32(v))

    def deliver(v, j):
        i = order[j]
        arrived(part_in.at[v, i, xi], pair_r.at[v, 0, i])
        arrived(xr.at[v, i], x_r.at[v, i])
        summed = (
            part[v, i, ci, xi].astype(F32) + part_in[v, i, xi].astype(F32) + xr[v, i].astype(F32)
        )
        inverse = invc[v, rowpos(pos), 0:1]
        speech = kindc[v, rowpos(pos), 0:1] > 0.5
        off = pl.multiple_of(lax.rem(i * cols, gcols), cols)
        pair = gain_all[i * cols // gcols, v, :, pl.ds(off, cols)].astype(F32)
        summed = inverse * jnp.where(speech, pair[1:2, :], pair[0:1, :]) * summed
        if j == 0:
            line = stat_s[v]
            arrived(stat_in.at[v], sp_r.at[v])
            for k in range(1, SUB):
                line = line + stat_in[v, k - 1]
            lane = lax.broadcasted_iota(jnp.int32, (rows, n), 1)
            row = lax.broadcasted_iota(jnp.int32, (rows, n), 0)
            pick = lane == row + pos * rows
            mean = jnp.sum(jnp.where(pick, line[0:1, :], 0.0), axis=1, keepdims=True) / width
            x = xg[v, t, rowpos(pos), :].astype(F32)
            summed = gr[v].astype(F32) + summed - x * (inverse * inverse * mean)
        zs[v, i] = summed.astype(BF16)
        goal = slot(v, here)
        send(zs.at[v, i], out.at[goal, t], z_s.at[0], z_r.at[goal], (before, i))

    def collect(v):
        goal = slot(v, section_after)
        arrived(out.at[goal], z_r.at[goal])

    def read_kinds():
        eye_r = lax.broadcasted_iota(jnp.int32, (rows, rows), 0) == lax.broadcasted_iota(
            jnp.int32, (rows, rows), 1
        )
        arrived(kinds.at[pl.ds(0, SUB - 1)], small_r.at[0])
        arrived(gain_all.at[pl.ds(0, SUB - 1)], small_r.at[1])
        for v in range(2):
            for p in range(SUB):
                line = kinds[p, v : v + 1, :].astype(F32)
                column = jnp.sum(jnp.where(eye_r, line, 0.0), axis=1, keepdims=True)
                kindc[v, p * rows : (p + 1) * rows, :] = jnp.broadcast_to(column, (rows, 128))

    take(1, 1)
    for j in range(2, T - 1):
        take(1, j)
    join_weights(1)
    take(1, T - 1)
    take_x(1, 0)
    take_x(0, 0)
    read_kinds()
    project(1, 0)
    for j in range(T - 1, 0, -1) if T - 1 <= 2 * reach[0] else range(1, T):
        take(0, j)
    join_weights(0)
    take_x(1, 1)
    for j in range(2, T):
        take_x(1, j)
    project(1, *range(1, T))
    share_keys(1)
    for j in range(T - 1, 0, -1):
        take_x(0, j)
    project(0, *range(T - 1, -1, -1))
    share_keys(0)
    hload.wait()
    grload.wait()
    attend(1)
    attend(0)
    joined = joined_grads(1)
    for j in range(T - 1, -1, -1):
        term(1, joined, j)
        if j < T - 1:
            cross(1, j + 1)
    cross(1, 0)
    share_stat(1)
    joined = joined_grads(0)
    for j in range(T - 1, -1, -1):
        term(0, joined, j)
        if j < T - 1:
            cross(0, j + 1)
            deliver(1, j + 1)
    cross(0, 0)
    share_stat(0)
    deliver(1, 0)
    for j in range(T - 1, -1, -1):
        deliver(0, j)

    for v in range(2):
        for ssem, inside, dev in own_ways(v):

            @pl.when(inside)
            def _():
                sent(xs.at[0, 0], ssem)

        if v in across_all:
            sent(xs.at[0], ag_s.at[ACROSS + v])
        else:
            sent(xs.at[0, 0], far_s.at[v, 0])
            for ssem, inside, dev in near_ways(v):

                @pl.when(inside)
                def _():
                    sent(xs.at[0, 0], ssem)

        for j in range(1, T):
            for ssem, use, dev in onward_ways(v, j):

                @pl.when(use)
                def _():
                    sent(xs.at[0, 0], ssem)

            if v not in across_all and j > 1:

                @pl.when(is_far(j))
                def _():
                    sent(xs.at[0, 0], far_s.at[v, j])

    sent(xs, ag_s.at[PAIR])
    sent(xs, ag_s.at[PAIR_X])
    sent(kinds.at[pl.ds(0, SUB - 1)], small_s.at[0])
    sent(gain_all.at[pl.ds(0, SUB - 1)], small_s.at[1])
    for v in range(2):
        sent(dkv_in.at[:, v], kv_s.at[v])
        sent(dkv_in.at[:, v], dk_s.at[v])
        sent(stat_z.at[v], st_s.at[v])
    for v in range(2):
        sent(stat_in.at[v], sp_s.at[v])
    sent(part_in, pair_s.at[0])
    sent(xs, x_s.at[0])
    sent(zs, z_s.at[0])
    collect(1)
    collect(0)


def per_device(sections, acts, grads_in, head_grads, types, gains, w_query, w_key, w_value):
    T = lax.axis_size("tensor")
    acts, grads_in, head_grads, types, gains = acts[0], grads_in[0], head_grads[0], types[0], gains[0]
    w_query, w_key, w_value = w_query[0], jnp.swapaxes(w_key[0], 1, 2), jnp.swapaxes(w_value[0], 1, 2)
    spans, rows, cols = acts.shape
    n = SUB * rows
    hd = w_query.shape[2]
    kc = w_key.shape[1]
    w_query = w_query.reshape(spans, T, cols, hd)
    V = pltpu.VMEM
    D = pltpu.SemaphoreType.DMA
    scratch = [
        V((2, T, n, cols), BF16), V((SUB, 2, rows), jnp.int32), V((SUB,) + gains.shape, BF16),
        V(w_key.shape, BF16), V(w_value.shape, BF16),
        V((2, T, cols, hd + 2 * kc), BF16), V(head_grads.shape, BF16), V(grads_in.shape, BF16),
        V((2, n, 128), F32), V((2, n, 128), F32), V((2, n, hd + 2 * kc), F32), V((2, n, 128), F32),
        V((2, 2, hd, n), BF16), V((2, 2, hd, n), BF16), V((T - 1, 2, 2, kc, n), BF16),
        V((2, 8, n), F32), V((2, T - 1, 8, n), F32), V((2, 8, n), F32), V((2, SUB - 1, 8, n), F32),
        V((2, T, 2, 2, rows, cols), BF16), V((2, T, 2, rows, cols), BF16),
        V((2, T, rows, cols), BF16), V((2, T, rows, cols), BF16), V((2, T, rows, cols), BF16),
        D((9,)), D((4,)), D((2, 3, 2)), D((2, 2)), D((2, T)), D((2, T, 1 if T <= 4 else 3)), D((2, 3, T)), D((2,)), D((2,)),
        D((2,)), D((2,)), D((2,)), D((2,)), D((2,)), D((2,)), D((2,)), D((2,)),
        D((1,)), D((2, 2, T)), D((1,)), D((2, T)), D((1,)), D((2,)),
    ]

    def body(*refs):
        kernel(sections, T, *refs)

    routed = pl.pallas_call(
        body,
        out_shape=jax.ShapeDtypeStruct((2, T, rows, cols), BF16),
        in_specs=[pl.BlockSpec(memory_space=pl.ANY)] * 8,
        out_specs=pl.BlockSpec(memory_space=pl.ANY),
        scratch_shapes=scratch,
        compiler_params=pltpu.CompilerParams(
            collective_id=0, has_side_effects=True, vmem_limit_bytes=67_000_000
        ),
        name="relay",
    )(acts, grads_in, head_grads, types, gains, w_query, w_key, w_value)
    return jnp.sum(routed.astype(F32), axis=1).astype(BF16)[None]


def solution(mesh):
    sections = mesh.shape["section"] // SUB

    def run(*args):
        return per_device(sections, *args)

    return jax.shard_map(
        run,
        mesh=mesh,
        in_specs=(
            P("section", None, None, "tensor"),
            P("section", None, None, "tensor"),
            P("section", None, None, "tensor"),
            P("section", None, None),
            P("section", None, None, None),
            P("section", None, None, "tensor"),
            P("section", None, None, "tensor"),
            P("section", None, None, "tensor"),
        ),
        out_specs=P("section", None, None, "tensor"),
        check_vma=False,
    )
```

```python
import jax
import jax.numpy as jnp
from jax import lax
from jax.experimental import pallas as pl
from jax.experimental.pallas import tpu as pltpu
from jax.sharding import PartitionSpec as P

SUB = 4
EPS = 1e-05
MESH = pl.DeviceIdType.MESH
F32 = jnp.float32
BF16 = jnp.bfloat16
ACROSS, PAIR, PAIR_X = 0, 2, 3
FROM_Z, FROM_X, FROM_PAIR = range(3)


def dot(a, b, dims):
    return lax.dot_general(a, b, (dims, ((), ())), preferred_element_type=F32)


def kernel(
    sections, tensors,
    acts, grads, heads, types, gains, wq, wk, wv,
    out,
    xg, kinds, gain_all, wkv, wvv, wcat, hg, gr, kindc, invc, acc, square,
    kvt, dkv, dkv_in, stat, stat_z, stat_s, stat_in,
    part, part_in, xs, xr, zs,
    loc, ag_s, own_s, near_s, far_s, relay_s, ag_r, small_s, small_r, kv_s, kv_r, dk_s, dk_r, st_s, st_r, sp_s, sp_r,
    pair_s, pair_r, x_s, x_r, z_s, z_r,
):
    spans, rows, cols = acts.shape
    n = SUB * rows
    hd = wq.shape[3]
    kc = wk.shape[1]
    width = cols * tensors
    gcols = gains.shape[2]
    T = tensors
    t = lax.axis_index("tensor")
    sec = lax.axis_index("section")
    pos = lax.rem(sec, SUB)
    here = sec // SUB
    base = here * SUB
    xi = pos // 2
    ci = lax.rem(pos, 2)
    pos_pair = xi * 2 + (1 - ci)
    pos_x = (1 - xi) * 2 + ci
    pos_diag = (1 - xi) * 2 + (1 - ci)
    pair_dev = (base + pos_pair, t)
    x_dev = (base + pos_x, t)
    section_before = lax.rem(here + sections - 1, sections)
    section_after = lax.rem(here + 1, sections)
    before = section_before * SUB + pos
    after = section_after * SUB + pos

    both = 2 * lax.min(t, T - 1 - t)
    order = [t]
    for j in range(1, T):
        d = (j + 1) // 2
        near = t - d if j % 2 else t + d
        rest = lax.select(2 * t < T - 1, jnp.int32(j), jnp.int32(T - 1 - j))
        order.append(lax.select(j <= both, near, rest))

    def pos_peer(k):
        return (base + lax.rem(pos + k, SUB), t)

    def z_peer(k):
        return (sec, lax.rem(t + k, T))

    def send(src, dst, ssem, rsem, dev):
        pltpu.make_async_remote_copy(
            src_ref=src, dst_ref=dst, send_sem=ssem, recv_sem=rsem, device_id=dev, device_id_type=MESH
        ).start()

    def sent(src, ssem):
        pltpu.make_async_copy(src, src, ssem).wait()

    def arrived(dst, rsem):
        pltpu.make_async_copy(dst, dst, rsem).wait()

    def rowpos(p):
        return pl.ds(pl.multiple_of(p * rows, rows), rows)

    def blk(v, p, tt):
        return xg.at[v, tt, rowpos(p), :]

    own = [pltpu.make_async_copy(acts.at[v], blk(v, pos, t), loc.at[v]) for v in range(2)]
    kload = pltpu.make_async_copy(types, kinds.at[pos], loc.at[2])
    gload = pltpu.make_async_copy(gains, gain_all.at[pos], loc.at[3])
    wload = [
        pltpu.make_async_copy(wk, wkv, loc.at[5]),
        pltpu.make_async_copy(wv, wvv, loc.at[6]),
    ]
    qload = pltpu.make_async_copy(wq, wcat.at[:, :, :, pl.ds(0, hd)], loc.at[4])
    hload = pltpu.make_async_copy(heads, hg, loc.at[7])
    grload = pltpu.make_async_copy(grads, gr, loc.at[8])
    for copy in own[::-1] + [kload, gload] + wload + [qload, hload, grload]:
        copy.start()

    barrier = pltpu.get_barrier_semaphore()
    greeted = [z_peer(k) for k in range(1, T)] + [pos_peer(k) for k in range(1, SUB)]
    greeted += [(before, lax.rem(t + k, T)) for k in range(T)]
    if sections > 2:
        greeted += [(after, lax.rem(t + k, T)) for k in range(T)]
    for dev in greeted:
        pl.semaphore_signal(barrier, inc=1, device_id=dev, device_id_type=MESH)
    pl.semaphore_wait(barrier, len(greeted))

    across_all = (1,)
    reach, nearest_first = (2, 2), (True, True)

    def pass_block(v, p, tt, ssem, kind, dev):
        send(blk(v, p, tt), blk(v, p, tt), ssem, ag_r.at[v, kind, tt], dev)

    def to_pair(v, p, tt):
        pass_block(v, p, tt, ag_s.at[PAIR if p is pos else PAIR_X], FROM_PAIR, pair_dev)

    def ways(*steps):
        for kind, step in steps:
            goal = t + step
            inside = goal >= 0 if step < 0 else goal < T
            yield kind, inside, (sec, lax.min(lax.max(goal, 0), T - 1))

    def own_ways(v):
        steps = range(1, reach[v] + 1)
        steps = steps if nearest_first[v] else steps[::-1]
        return ways(*((own_s.at[v, d - 1, side], (d, -d)[side]) for d in steps for side in range(2)))

    def near_ways(v):
        return ways((near_s.at[v, 0], -1), (near_s.at[v, 1], 1))

    def along(v):
        for ssem, inside, dev in own_ways(v):

            @pl.when(inside)
            def _():
                pass_block(v, pos, t, ssem, FROM_Z, dev)

    def onward_ways(v, j):
        tt, most = order[j], reach[v]
        away = lax.select(tt < t, jnp.int32(1), jnp.int32(-1))
        turn = lax.rem((t - tt) * away, most) == 0
        for step in range(1, most + 1):
            if not any(d % most == 0 and d + step < T for d in range((j + 1) // 2, j + 1)):
                continue
            goal = t + step * away
            use = jnp.logical_and(turn, jnp.logical_and(goal >= 0, goal < T))
            yield relay_s.at[v, 0 if T <= 4 else j, step - 1], use, (sec, lax.min(lax.max(goal, 0), T - 1))

    def is_far(j):
        return jnp.abs(order[j] - t) > 1

    def take(v, j):
        tt = order[j]
        arrived(blk(v, pos, tt), ag_r.at[v, FROM_Z, tt])
        for ssem, use, dev in onward_ways(v, j):

            @pl.when(use)
            def _():
                pass_block(v, pos, tt, ssem, FROM_Z, dev)

        if v in across_all:
            pass_block(v, pos, tt, ag_s.at[ACROSS + v], FROM_X, x_dev)
        elif j > 1:

            @pl.when(is_far(j))
            def _():
                pass_block(v, pos, tt, far_s.at[v, j], FROM_X, x_dev)

        to_pair(v, pos, tt)

    def take_x(v, j):
        tt = order[j]
        arrived(blk(v, pos_x, tt), ag_r.at[v, FROM_X, tt])
        if v not in across_all and j == 0:
            for ssem, inside, dev in near_ways(v):

                @pl.when(inside)
                def _():
                    pass_block(v, pos_x, tt, ssem, FROM_X, dev)

        to_pair(v, pos_x, tt)

    def across(v):
        pass_block(v, pos, t, ag_s.at[ACROSS + v] if v in across_all else far_s.at[v, 0], FROM_X, x_dev)

    own[1].wait()
    across(1)
    along(1)
    own[0].wait()
    across(0)
    along(0)
    to_pair(1, pos, t)
    to_pair(0, pos, t)
    kload.wait()
    gload.wait()
    for k in range(1, SUB):
        send(kinds.at[pos], kinds.at[pos], small_s.at[0], small_r.at[0], pos_peer(k))
        send(gain_all.at[pos], gain_all.at[pos], small_s.at[1], small_r.at[1], pos_peer(k))

    for copy in wload:
        copy.wait()
    qload.wait()

    def join_weights(v):
        for i in range(T):
            at = pl.ds(i * cols, cols)
            kv_cols = jnp.concatenate([wkv[v, :, at], wvv[v, :, at]], axis=0)
            wcat[v, i, :, hd:] = jnp.transpose(kv_cols)

    def project(v, *blocks):
        for j in blocks:
            arrived(xs.at[0, pl.ds(0, 2)], ag_r.at[v, FROM_PAIR, order[j]])
        speech = kindc[v, :, 0:1] > 0.5
        squares, product = None, None
        for j in blocks:
            tt = order[j]
            block = tt * cols // gcols
            off = pl.multiple_of(lax.rem(tt * cols, gcols), cols)
            pair = gain_all[block, v, :, pl.ds(off, cols)].astype(F32)
            xf = xg[v, tt].astype(F32)
            square_j = jnp.sum(xf * xf, axis=1, keepdims=True)
            scaled = (xf * jnp.where(speech, pair[1:2, :], pair[0:1, :])).astype(BF16)
            product_j = dot(scaled, wcat[v, tt], ((1,), (0,)))
            squares = square_j if squares is None else squares + square_j
            product = product_j if product is None else product + product_j
        squares = jnp.broadcast_to(squares, (n, 128))
        if 0 in blocks:
            square[v] = squares
            acc[v] = product
        else:
            square[v] += squares
            acc[v] += product

    mine = pl.ds(pl.multiple_of(t * kc, kc), kc)
    queries = [None, None]

    def share_keys(v):
        inverse = lax.rsqrt(square[v][:, 0:1] / width + EPS)
        invc[v] = jnp.broadcast_to(inverse, (n, 128))
        projected = acc[v] * inverse
        turned = jnp.transpose(projected[:, hd:]).astype(BF16)
        kvt[v, 0, mine, :] = turned[:kc]
        kvt[v, 1, mine, :] = turned[kc:]
        for k in range(1, T):
            block = kvt.at[v, :, mine, :]
            send(block, block, kv_s.at[v], kv_r.at[v], z_peer(k))
        queries[v] = projected[:, :hd].astype(BF16)

    scale = hd ** (-0.5)
    query_grads = [None, None]

    def attend(v):
        eye = lax.broadcasted_iota(jnp.int32, (n, n), 0) == lax.broadcasted_iota(jnp.int32, (n, n), 1)
        causal = lax.broadcasted_iota(jnp.int32, (n, n), 0) >= lax.broadcasted_iota(
            jnp.int32, (n, n), 1
        )
        arrived(dkv_in.at[:, v], kv_r.at[v])
        kt = kvt[v, 0]
        vt = kvt[v, 1]
        og = hg[v]
        scores = dot(queries[v], kt, ((1,), (0,))) * scale
        scores = jnp.where(causal, scores, -1e30)
        top = jnp.max(scores, axis=1, keepdims=True)
        weights = jnp.exp(scores - top)
        probs = weights / jnp.sum(weights, axis=1, keepdims=True)
        pg = dot(og, vt, ((1,), (0,)))
        sg = probs * (pg - jnp.sum(pg * probs, axis=1, keepdims=True)) * scale
        sg = sg.astype(BF16)
        key_each = dot(queries[v], sg, ((0,), (0,)))
        value_each = dot(og, probs.astype(BF16), ((0,), (0,)))
        dkv[v, 0] = key_each.astype(BF16)
        dkv[v, 1] = value_each.astype(BF16)
        for k in range(1, T):
            goal = pl.ds(pl.multiple_of(lax.rem(t + k, T) * kc, kc), kc)
            send(dkv.at[v, :, goal, :], dkv_in.at[k - 1, v], dk_s.at[v], dk_r.at[v], z_peer(k))
        qg = dot(sg, kt, ((1,), (1,)))
        query_grads[v] = qg.astype(BF16)
        column = jnp.sum(qg * queries[v].astype(F32), axis=1, keepdims=True)
        line = jnp.sum(jnp.where(eye, column, 0.0), axis=0, keepdims=True)
        line = line + jnp.sum(
            key_each * kt.astype(F32) + value_each * vt.astype(F32), axis=0, keepdims=True
        )
        stat[v] = jnp.broadcast_to(line, (8, n))
        for k in range(1, T):
            send(stat.at[v], stat_z.at[v, k - 1], st_s.at[v], st_r.at[v], z_peer(k))

    def share_stat(v):
        line = stat[v]
        arrived(stat_z.at[v], st_r.at[v])
        for k in range(1, T):
            line = line + stat_z[v, k - 1]
        stat_s[v] = line
        for k in range(1, SUB):
            send(stat_s.at[v], stat_in.at[v, k - 1], sp_s.at[v], sp_r.at[v], pos_peer(k))

    def joined_grads(v):
        summed = dkv[v, :, mine, :].astype(F32)
        arrived(dkv_in.at[:, v], dk_r.at[v])
        for k in range(1, T):
            summed = summed + dkv_in[k - 1, v].astype(F32)
        kv_rows = jnp.transpose(summed.reshape(2 * kc, n)).astype(BF16)
        return jnp.concatenate([query_grads[v], kv_rows], axis=1)

    def term(v, joined, j):
        i = order[j]
        piece = dot(joined, wcat[v, i], ((1,), (1,))).astype(BF16)
        for p in range(SUB):
            part[v, i, p % 2, p // 2] = piece[p * rows : (p + 1) * rows]
        for x in (1 - xi, xi):
            kind = lax.rem(x + xi, 2)
            send(part.at[v, i, 1 - ci, x], part_in.at[v, i, x], pair_s.at[0], pair_r.at[v, kind, i], pair_dev)

    def cross(v, j):
        i = order[j]
        arrived(part_in.at[v, i, 1 - xi], pair_r.at[v, 1, i])
        xs[v, i] = (part[v, i, ci, 1 - xi].astype(F32) + part_in[v, i, 1 - xi].astype(F32)).astype(BF16)
        send(xs.at[v, i], xr.at[v, i], x_s.at[0], x_r.at[v, i], x_dev)

    def slot(v, section):
        return lax.select(section == 0, jnp.int32(1 - v), jnp.int32(v))

    def deliver(v, j):
        i = order[j]
        arrived(part_in.at[v, i, xi], pair_r.at[v, 0, i])
        arrived(xr.at[v, i], x_r.at[v, i])
        summed = (
            part[v, i, ci, xi].astype(F32) + part_in[v, i, xi].astype(F32) + xr[v, i].astype(F32)
        )
        inverse = invc[v, rowpos(pos), 0:1]
        speech = kindc[v, rowpos(pos), 0:1] > 0.5
        off = pl.multiple_of(lax.rem(i * cols, gcols), cols)
        pair = gain_all[i * cols // gcols, v, :, pl.ds(off, cols)].astype(F32)
        summed = inverse * jnp.where(speech, pair[1:2, :], pair[0:1, :]) * summed
        if j == 0:
            line = stat_s[v]
            arrived(stat_in.at[v], sp_r.at[v])
            for k in range(1, SUB):
                line = line + stat_in[v, k - 1]
            lane = lax.broadcasted_iota(jnp.int32, (rows, n), 1)
            row = lax.broadcasted_iota(jnp.int32, (rows, n), 0)
            pick = lane == row + pos * rows
            mean = jnp.sum(jnp.where(pick, line[0:1, :], 0.0), axis=1, keepdims=True) / width
            x = xg[v, t, rowpos(pos), :].astype(F32)
            summed = gr[v].astype(F32) + summed - x * (inverse * inverse * mean)
        zs[v, i] = summed.astype(BF16)
        goal = slot(v, here)
        send(zs.at[v, i], out.at[goal, t], z_s.at[0], z_r.at[goal], (before, i))

    def collect(v):
        goal = slot(v, section_after)
        arrived(out.at[goal], z_r.at[goal])

    def read_kinds():
        eye_r = lax.broadcasted_iota(jnp.int32, (rows, rows), 0) == lax.broadcasted_iota(
            jnp.int32, (rows, rows), 1
        )
        arrived(kinds.at[pl.ds(0, SUB - 1)], small_r.at[0])
        arrived(gain_all.at[pl.ds(0, SUB - 1)], small_r.at[1])
        for v in range(2):
            for p in range(SUB):
                line = kinds[p, v : v + 1, :].astype(F32)
                column = jnp.sum(jnp.where(eye_r, line, 0.0), axis=1, keepdims=True)
                kindc[v, p * rows : (p + 1) * rows, :] = jnp.broadcast_to(column, (rows, 128))

    take(1, 1)
    for j in range(2, T - 1):
        take(1, j)
    join_weights(1)
    join_weights(0)
    take(1, T - 1)
    take_x(1, 0)
    take_x(0, 0)
    read_kinds()
    project(1, 0)
    for j in range(1, T):
        take(0, j)
    take_x(1, 1)
    for j in range(2, T):
        take_x(1, j)
    project(1, *range(1, T))
    share_keys(1)
    for j in range(T - 1, 0, -1):
        take_x(0, j)
    project(0, *range(T - 1, -1, -1))
    share_keys(0)
    hload.wait()
    grload.wait()
    attend(1)
    attend(0)
    share_stat(1)
    joined = joined_grads(1)
    for j in range(T - 1, -1, -1):
        term(1, joined, j)
        if j < T - 1:
            cross(1, j + 1)
    cross(1, 0)
    joined = joined_grads(0)
    for j in range(T - 1, -1, -1):
        term(0, joined, j)
        if j < T - 1:
            cross(0, j + 1)
            deliver(1, j + 1)
    cross(0, 0)
    share_stat(0)
    deliver(1, 0)
    for j in range(T - 1, -1, -1):
        deliver(0, j)

    for v in range(2):
        for ssem, inside, dev in own_ways(v):

            @pl.when(inside)
            def _():
                sent(xs.at[0, 0], ssem)

        if v in across_all:
            sent(xs.at[0], ag_s.at[ACROSS + v])
        else:
            sent(xs.at[0, 0], far_s.at[v, 0])
            for ssem, inside, dev in near_ways(v):

                @pl.when(inside)
                def _():
                    sent(xs.at[0, 0], ssem)

        for j in range(1, T):
            for ssem, use, dev in onward_ways(v, j):

                @pl.when(use)
                def _():
                    sent(xs.at[0, 0], ssem)

            if v not in across_all and j > 1:

                @pl.when(is_far(j))
                def _():
                    sent(xs.at[0, 0], far_s.at[v, j])

    sent(xs, ag_s.at[PAIR])
    sent(xs, ag_s.at[PAIR_X])
    sent(kinds.at[pl.ds(0, SUB - 1)], small_s.at[0])
    sent(gain_all.at[pl.ds(0, SUB - 1)], small_s.at[1])
    for v in range(2):
        sent(dkv_in.at[:, v], kv_s.at[v])
        sent(dkv_in.at[:, v], dk_s.at[v])
        sent(stat_z.at[v], st_s.at[v])
    for v in range(2):
        sent(stat_in.at[v], sp_s.at[v])
    sent(part_in, pair_s.at[0])
    sent(xs, x_s.at[0])
    sent(zs, z_s.at[0])
    collect(1)
    collect(0)


def per_device(sections, acts, grads_in, head_grads, types, gains, w_query, w_key, w_value):
    T = lax.axis_size("tensor")
    acts, grads_in, head_grads, types, gains = acts[0], grads_in[0], head_grads[0], types[0], gains[0]
    w_query, w_key, w_value = w_query[0], jnp.swapaxes(w_key[0], 1, 2), jnp.swapaxes(w_value[0], 1, 2)
    spans, rows, cols = acts.shape
    n = SUB * rows
    hd = w_query.shape[2]
    kc = w_key.shape[1]
    w_query = w_query.reshape(spans, T, cols, hd)
    V = pltpu.VMEM
    D = pltpu.SemaphoreType.DMA
    scratch = [
        V((2, T, n, cols), BF16), V((SUB, 2, rows), jnp.int32), V((SUB,) + gains.shape, BF16),
        V(w_key.shape, BF16), V(w_value.shape, BF16),
        V((2, T, cols, hd + 2 * kc), BF16), V(head_grads.shape, BF16), V(grads_in.shape, BF16),
        V((2, n, 128), F32), V((2, n, 128), F32), V((2, n, hd + 2 * kc), F32), V((2, n, 128), F32),
        V((2, 2, hd, n), BF16), V((2, 2, hd, n), BF16), V((T - 1, 2, 2, kc, n), BF16),
        V((2, 8, n), F32), V((2, T - 1, 8, n), F32), V((2, 8, n), F32), V((2, SUB - 1, 8, n), F32),
        V((2, T, 2, 2, rows, cols), BF16), V((2, T, 2, rows, cols), BF16),
        V((2, T, rows, cols), BF16), V((2, T, rows, cols), BF16), V((2, T, rows, cols), BF16),
        D((9,)), D((4,)), D((2, 2, 2)), D((1, 2)), D((1, T)), D((2, 1, 1) if T <= 4 else (2, T, 2)), D((2, 3, T)), D((2,)), D((2,)),
        D((2,)), D((2,)), D((2,)), D((2,)), D((2,)), D((2,)), D((2,)), D((2,)),
        D((1,)), D((2, 2, T)), D((1,)), D((2, T)), D((1,)), D((2,)),
    ]

    def body(*refs):
        kernel(sections, T, *refs)

    routed = pl.pallas_call(
        body,
        out_shape=jax.ShapeDtypeStruct((2, T, rows, cols), BF16),
        in_specs=[pl.BlockSpec(memory_space=pl.ANY)] * 8,
        out_specs=pl.BlockSpec(memory_space=pl.ANY),
        scratch_shapes=scratch,
        compiler_params=pltpu.CompilerParams(
            collective_id=0, has_side_effects=True, vmem_limit_bytes=67_000_000
        ),
        name="relay",
    )(acts, grads_in, head_grads, types, gains, w_query, w_key, w_value)
    return jnp.sum(routed.astype(F32), axis=1).astype(BF16)[None]


def solution(mesh):
    sections = mesh.shape["section"] // SUB

    def run(*args):
        return per_device(sections, *args)

    return jax.shard_map(
        run,
        mesh=mesh,
        in_specs=(
            P("section", None, None, "tensor"),
            P("section", None, None, "tensor"),
            P("section", None, None, "tensor"),
            P("section", None, None),
            P("section", None, None, None),
            P("section", None, None, "tensor"),
            P("section", None, None, "tensor"),
            P("section", None, None, "tensor"),
        ),
        out_specs=P("section", None, None, "tensor"),
        check_vma=False,
    )
```

```python
import jax
import jax.numpy as jnp
from jax import lax
from jax.experimental import pallas as pl
from jax.experimental.pallas import tpu as pltpu
from jax.sharding import PartitionSpec as P

SUB = 4
EPS = 1e-05
MESH = pl.DeviceIdType.MESH
F32 = jnp.float32
BF16 = jnp.bfloat16
ACROSS, PAIR, PAIR_X = 0, 2, 3
FROM_Z, FROM_X, FROM_PAIR = range(3)


def dot(a, b, dims):
    return lax.dot_general(a, b, (dims, ((), ())), preferred_element_type=F32)


def kernel(
    sections, tensors,
    acts, grads, heads, types, gains, wq, wk, wv,
    out,
    xg, kinds, gain_all, wkv, wvv, wcat, hg, gr, kindc, invc, acc, square,
    kvt, dkv, dkv_in, stat, stat_z, stat_s, stat_in,
    part, part_in, xs, xr, zs,
    loc, ag_s, own_s, near_s, far_s, relay_s, ag_r, small_s, small_r, kv_s, kv_r, dk_s, dk_r, st_s, st_r, sp_s, sp_r,
    pair_s, pair_r, x_s, x_r, z_s, z_r,
):
    spans, rows, cols = acts.shape
    n = SUB * rows
    hd = wq.shape[3]
    kc = wk.shape[1]
    width = cols * tensors
    gcols = gains.shape[2]
    T = tensors
    t = lax.axis_index("tensor")
    sec = lax.axis_index("section")
    pos = lax.rem(sec, SUB)
    here = sec // SUB
    base = here * SUB
    xi = pos // 2
    ci = lax.rem(pos, 2)
    pos_pair = xi * 2 + (1 - ci)
    pos_x = (1 - xi) * 2 + ci
    pos_diag = (1 - xi) * 2 + (1 - ci)
    pair_dev = (base + pos_pair, t)
    x_dev = (base + pos_x, t)
    section_before = lax.rem(here + sections - 1, sections)
    section_after = lax.rem(here + 1, sections)
    before = section_before * SUB + pos
    after = section_after * SUB + pos

    both = 2 * lax.min(t, T - 1 - t)
    order = [t]
    for j in range(1, T):
        d = (j + 1) // 2
        near = t - d if j % 2 else t + d
        rest = lax.select(2 * t < T - 1, jnp.int32(j), jnp.int32(T - 1 - j))
        order.append(lax.select(j <= both, near, rest))

    def pos_peer(k):
        return (base + lax.rem(pos + k, SUB), t)

    def z_peer(k):
        return (sec, lax.rem(t + k, T))

    def send(src, dst, ssem, rsem, dev):
        pltpu.make_async_remote_copy(
            src_ref=src, dst_ref=dst, send_sem=ssem, recv_sem=rsem, device_id=dev, device_id_type=MESH
        ).start()

    def sent(src, ssem):
        pltpu.make_async_copy(src, src, ssem).wait()

    def arrived(dst, rsem):
        pltpu.make_async_copy(dst, dst, rsem).wait()

    def rowpos(p):
        return pl.ds(pl.multiple_of(p * rows, rows), rows)

    def blk(v, p, tt):
        return xg.at[v, tt, rowpos(p), :]

    own = [pltpu.make_async_copy(acts.at[v], blk(v, pos, t), loc.at[v]) for v in range(2)]
    kload = pltpu.make_async_copy(types, kinds.at[pos], loc.at[2])
    gload = pltpu.make_async_copy(gains, gain_all.at[pos], loc.at[3])
    wload = [
        pltpu.make_async_copy(wk, wkv, loc.at[5]),
        pltpu.make_async_copy(wv, wvv, loc.at[6]),
    ]
    qload = pltpu.make_async_copy(wq, wcat.at[:, :, :, pl.ds(0, hd)], loc.at[4])
    hload = pltpu.make_async_copy(heads, hg, loc.at[7])
    grload = pltpu.make_async_copy(grads, gr, loc.at[8])
    for copy in own[::-1] + [kload, gload] + wload + [qload, hload, grload]:
        copy.start()

    barrier = pltpu.get_barrier_semaphore()
    greeted = [z_peer(k) for k in range(1, T)] + [pos_peer(k) for k in range(1, SUB)]
    greeted += [(before, lax.rem(t + k, T)) for k in range(T)]
    if sections > 2:
        greeted += [(after, lax.rem(t + k, T)) for k in range(T)]
    for dev in greeted:
        pl.semaphore_signal(barrier, inc=1, device_id=dev, device_id_type=MESH)
    pl.semaphore_wait(barrier, len(greeted))

    across_all = (1,)
    reach, nearest_first = (2, 2), (True, True)

    def pass_block(v, p, tt, ssem, kind, dev):
        send(blk(v, p, tt), blk(v, p, tt), ssem, ag_r.at[v, kind, tt], dev)

    def to_pair(v, p, tt):
        pass_block(v, p, tt, ag_s.at[PAIR if p is pos else PAIR_X], FROM_PAIR, pair_dev)

    def ways(*steps):
        for kind, step in steps:
            goal = t + step
            inside = goal >= 0 if step < 0 else goal < T
            yield kind, inside, (sec, lax.min(lax.max(goal, 0), T - 1))

    def own_ways(v):
        steps = range(1, reach[v] + 1)
        steps = steps if nearest_first[v] else steps[::-1]
        return ways(*((own_s.at[v, d - 1, side], (d, -d)[side]) for d in steps for side in range(2)))

    def near_ways(v):
        return ways((near_s.at[v, 0], -1), (near_s.at[v, 1], 1))

    def along(v):
        for ssem, inside, dev in own_ways(v):

            @pl.when(inside)
            def _():
                pass_block(v, pos, t, ssem, FROM_Z, dev)

    def onward_ways(v, j):
        tt, most = order[j], reach[v]
        away = lax.select(tt < t, jnp.int32(1), jnp.int32(-1))
        turn = lax.rem((t - tt) * away, most) == 0
        for step in range(1, most + 1):
            if not any(d % most == 0 and d + step < T for d in range((j + 1) // 2, j + 1)):
                continue
            goal = t + step * away
            use = jnp.logical_and(turn, jnp.logical_and(goal >= 0, goal < T))
            yield relay_s.at[v, 0 if T <= 4 else j, step - 1], use, (sec, lax.min(lax.max(goal, 0), T - 1))

    def is_far(j):
        return jnp.abs(order[j] - t) > 1

    def take(v, j):
        tt = order[j]
        arrived(blk(v, pos, tt), ag_r.at[v, FROM_Z, tt])
        for ssem, use, dev in onward_ways(v, j):

            @pl.when(use)
            def _():
                pass_block(v, pos, tt, ssem, FROM_Z, dev)

        if v in across_all:
            pass_block(v, pos, tt, ag_s.at[ACROSS + v], FROM_X, x_dev)
        elif j > 1:

            @pl.when(is_far(j))
            def _():
                pass_block(v, pos, tt, far_s.at[v, j], FROM_X, x_dev)

        to_pair(v, pos, tt)

    def take_x(v, j):
        tt = order[j]
        arrived(blk(v, pos_x, tt), ag_r.at[v, FROM_X, tt])
        if v not in across_all and j == 0:
            for ssem, inside, dev in near_ways(v):

                @pl.when(inside)
                def _():
                    pass_block(v, pos_x, tt, ssem, FROM_X, dev)

        to_pair(v, pos_x, tt)

    def across(v):
        pass_block(v, pos, t, ag_s.at[ACROSS + v] if v in across_all else far_s.at[v, 0], FROM_X, x_dev)

    own[1].wait()
    across(1)
    along(1)
    own[0].wait()
    across(0)
    along(0)
    to_pair(1, pos, t)
    to_pair(0, pos, t)
    kload.wait()
    gload.wait()
    for k in range(1, SUB):
        send(kinds.at[pos], kinds.at[pos], small_s.at[0], small_r.at[0], pos_peer(k))
        send(gain_all.at[pos], gain_all.at[pos], small_s.at[1], small_r.at[1], pos_peer(k))

    for copy in wload:
        copy.wait()
    qload.wait()

    def join_weights(v):
        for i in range(T):
            at = pl.ds(i * cols, cols)
            kv_cols = jnp.concatenate([wkv[v, :, at], wvv[v, :, at]], axis=0)
            wcat[v, i, :, hd:] = jnp.transpose(kv_cols)

    def project(v, *blocks):
        for j in blocks:
            arrived(xs.at[0, pl.ds(0, 2)], ag_r.at[v, FROM_PAIR, order[j]])
        speech = kindc[v, :, 0:1] > 0.5
        squares, product = None, None
        for j in blocks:
            tt = order[j]
            block = tt * cols // gcols
            off = pl.multiple_of(lax.rem(tt * cols, gcols), cols)
            pair = gain_all[block, v, :, pl.ds(off, cols)].astype(F32)
            xf = xg[v, tt].astype(F32)
            square_j = jnp.sum(xf * xf, axis=1, keepdims=True)
            scaled = (xf * jnp.where(speech, pair[1:2, :], pair[0:1, :])).astype(BF16)
            product_j = dot(scaled, wcat[v, tt], ((1,), (0,)))
            squares = square_j if squares is None else squares + square_j
            product = product_j if product is None else product + product_j
        squares = jnp.broadcast_to(squares, (n, 128))
        if 0 in blocks:
            square[v] = squares
            acc[v] = product
        else:
            square[v] += squares
            acc[v] += product

    mine = pl.ds(pl.multiple_of(t * kc, kc), kc)
    queries = [None, None]

    def share_keys(v):
        inverse = lax.rsqrt(square[v][:, 0:1] / width + EPS)
        invc[v] = jnp.broadcast_to(inverse, (n, 128))
        projected = acc[v] * inverse
        turned = jnp.transpose(projected[:, hd:]).astype(BF16)
        kvt[v, 0, mine, :] = turned[:kc]
        kvt[v, 1, mine, :] = turned[kc:]
        for k in range(1, T):
            block = kvt.at[v, :, mine, :]
            send(block, block, kv_s.at[v], kv_r.at[v], z_peer(k))
        queries[v] = projected[:, :hd].astype(BF16)

    scale = hd ** (-0.5)
    query_grads = [None, None]

    def attend(v):
        eye = lax.broadcasted_iota(jnp.int32, (n, n), 0) == lax.broadcasted_iota(jnp.int32, (n, n), 1)
        causal = lax.broadcasted_iota(jnp.int32, (n, n), 0) >= lax.broadcasted_iota(
            jnp.int32, (n, n), 1
        )
        arrived(dkv_in.at[:, v], kv_r.at[v])
        kt = kvt[v, 0]
        vt = kvt[v, 1]
        og = hg[v]
        scores = dot(queries[v], kt, ((1,), (0,))) * scale
        scores = jnp.where(causal, scores, -1e30)
        top = jnp.max(scores, axis=1, keepdims=True)
        weights = jnp.exp(scores - top)
        probs = weights / jnp.sum(weights, axis=1, keepdims=True)
        pg = dot(og, vt, ((1,), (0,)))
        sg = probs * (pg - jnp.sum(pg * probs, axis=1, keepdims=True)) * scale
        sg = sg.astype(BF16)
        key_each = dot(queries[v], sg, ((0,), (0,)))
        value_each = dot(og, probs.astype(BF16), ((0,), (0,)))
        dkv[v, 0] = key_each.astype(BF16)
        dkv[v, 1] = value_each.astype(BF16)
        for k in range(1, T):
            goal = pl.ds(pl.multiple_of(lax.rem(t + k, T) * kc, kc), kc)
            send(dkv.at[v, :, goal, :], dkv_in.at[k - 1, v], dk_s.at[v], dk_r.at[v], z_peer(k))
        qg = dot(sg, kt, ((1,), (1,)))
        query_grads[v] = qg.astype(BF16)
        column = jnp.sum(qg * queries[v].astype(F32), axis=1, keepdims=True)
        line = jnp.sum(jnp.where(eye, column, 0.0), axis=0, keepdims=True)
        line = line + jnp.sum(
            key_each * kt.astype(F32) + value_each * vt.astype(F32), axis=0, keepdims=True
        )
        stat[v] = jnp.broadcast_to(line, (8, n))
        for k in range(1, T):
            send(stat.at[v], stat_z.at[v, k - 1], st_s.at[v], st_r.at[v], z_peer(k))

    def share_stat(v):
        line = stat[v]
        arrived(stat_z.at[v], st_r.at[v])
        for k in range(1, T):
            line = line + stat_z[v, k - 1]
        stat_s[v] = line
        for k in range(1, SUB):
            send(stat_s.at[v], stat_in.at[v, k - 1], sp_s.at[v], sp_r.at[v], pos_peer(k))

    def joined_grads(v):
        summed = dkv[v, :, mine, :].astype(F32)
        arrived(dkv_in.at[:, v], dk_r.at[v])
        for k in range(1, T):
            summed = summed + dkv_in[k - 1, v].astype(F32)
        kv_rows = jnp.transpose(summed.reshape(2 * kc, n)).astype(BF16)
        return jnp.concatenate([query_grads[v], kv_rows], axis=1)

    def term(v, joined, j):
        i = order[j]
        piece = dot(joined, wcat[v, i], ((1,), (1,))).astype(BF16)
        for p in range(SUB):
            part[v, i, p % 2, p // 2] = piece[p * rows : (p + 1) * rows]
        for x in (1 - xi, xi):
            kind = lax.rem(x + xi, 2)
            send(part.at[v, i, 1 - ci, x], part_in.at[v, i, x], pair_s.at[0], pair_r.at[v, kind, i], pair_dev)

    def cross(v, j):
        i = order[j]
        arrived(part_in.at[v, i, 1 - xi], pair_r.at[v, 1, i])
        xs[v, i] = (part[v, i, ci, 1 - xi].astype(F32) + part_in[v, i, 1 - xi].astype(F32)).astype(BF16)
        send(xs.at[v, i], xr.at[v, i], x_s.at[0], x_r.at[v, i], x_dev)

    def slot(v, section):
        return lax.select(section == 0, jnp.int32(1 - v), jnp.int32(v))

    def deliver(v, j):
        i = order[j]
        arrived(part_in.at[v, i, xi], pair_r.at[v, 0, i])
        arrived(xr.at[v, i], x_r.at[v, i])
        summed = (
            part[v, i, ci, xi].astype(F32) + part_in[v, i, xi].astype(F32) + xr[v, i].astype(F32)
        )
        inverse = invc[v, rowpos(pos), 0:1]
        speech = kindc[v, rowpos(pos), 0:1] > 0.5
        off = pl.multiple_of(lax.rem(i * cols, gcols), cols)
        pair = gain_all[i * cols // gcols, v, :, pl.ds(off, cols)].astype(F32)
        summed = inverse * jnp.where(speech, pair[1:2, :], pair[0:1, :]) * summed
        if j == 0:
            line = stat_s[v]
            arrived(stat_in.at[v], sp_r.at[v])
            for k in range(1, SUB):
                line = line + stat_in[v, k - 1]
            lane = lax.broadcasted_iota(jnp.int32, (rows, n), 1)
            row = lax.broadcasted_iota(jnp.int32, (rows, n), 0)
            pick = lane == row + pos * rows
            mean = jnp.sum(jnp.where(pick, line[0:1, :], 0.0), axis=1, keepdims=True) / width
            x = xg[v, t, rowpos(pos), :].astype(F32)
            summed = gr[v].astype(F32) + summed - x * (inverse * inverse * mean)
        zs[v, i] = summed.astype(BF16)
        goal = slot(v, here)
        send(zs.at[v, i], out.at[goal, t], z_s.at[0], z_r.at[goal], (before, i))

    def collect(v):
        goal = slot(v, section_after)
        arrived(out.at[goal], z_r.at[goal])

    def read_kinds():
        eye_r = lax.broadcasted_iota(jnp.int32, (rows, rows), 0) == lax.broadcasted_iota(
            jnp.int32, (rows, rows), 1
        )
        arrived(kinds.at[pl.ds(0, SUB - 1)], small_r.at[0])
        arrived(gain_all.at[pl.ds(0, SUB - 1)], small_r.at[1])
        for v in range(2):
            for p in range(SUB):
                line = kinds[p, v : v + 1, :].astype(F32)
                column = jnp.sum(jnp.where(eye_r, line, 0.0), axis=1, keepdims=True)
                kindc[v, p * rows : (p + 1) * rows, :] = jnp.broadcast_to(column, (rows, 128))

    take(1, 1)
    for j in range(2, T - 1):
        take(1, j)
    join_weights(1)
    join_weights(0)
    take(1, T - 1)
    take_x(0, 0)
    take_x(1, 0)
    read_kinds()
    project(1, 0)
    for j in range(1, T):
        take(0, j)
    take_x(1, 1)
    for j in range(2, T):
        take_x(1, j)
    project(1, *range(1, T))
    share_keys(1)
    for j in range(T - 1, 0, -1):
        take_x(0, j)
    project(0, *range(T - 1, -1, -1))
    share_keys(0)
    hload.wait()
    grload.wait()
    attend(1)
    attend(0)
    share_stat(1)
    joined = joined_grads(1)
    for j in range(T - 1, -1, -1):
        term(1, joined, j)
        if j < T - 1:
            cross(1, j + 1)
    cross(1, 0)
    joined = joined_grads(0)
    for j in range(T - 1, -1, -1):
        term(0, joined, j)
        if j < T - 1:
            cross(0, j + 1)
            deliver(1, j + 1)
    cross(0, 0)
    share_stat(0)
    deliver(1, 0)
    for j in range(T - 1, -1, -1):
        deliver(0, j)

    for v in range(2):
        for ssem, inside, dev in own_ways(v):

            @pl.when(inside)
            def _():
                sent(xs.at[0, 0], ssem)

        if v in across_all:
            sent(xs.at[0], ag_s.at[ACROSS + v])
        else:
            sent(xs.at[0, 0], far_s.at[v, 0])
            for ssem, inside, dev in near_ways(v):

                @pl.when(inside)
                def _():
                    sent(xs.at[0, 0], ssem)

        for j in range(1, T):
            for ssem, use, dev in onward_ways(v, j):

                @pl.when(use)
                def _():
                    sent(xs.at[0, 0], ssem)

            if v not in across_all and j > 1:

                @pl.when(is_far(j))
                def _():
                    sent(xs.at[0, 0], far_s.at[v, j])

    sent(xs, ag_s.at[PAIR])
    sent(xs, ag_s.at[PAIR_X])
    sent(kinds.at[pl.ds(0, SUB - 1)], small_s.at[0])
    sent(gain_all.at[pl.ds(0, SUB - 1)], small_s.at[1])
    for v in range(2):
        sent(dkv_in.at[:, v], kv_s.at[v])
        sent(dkv_in.at[:, v], dk_s.at[v])
        sent(stat_z.at[v], st_s.at[v])
    for v in range(2):
        sent(stat_in.at[v], sp_s.at[v])
    sent(part_in, pair_s.at[0])
    sent(xs, x_s.at[0])
    sent(zs, z_s.at[0])
    collect(1)
    collect(0)


def per_device(sections, acts, grads_in, head_grads, types, gains, w_query, w_key, w_value):
    T = lax.axis_size("tensor")
    acts, grads_in, head_grads, types, gains = acts[0], grads_in[0], head_grads[0], types[0], gains[0]
    w_query, w_key, w_value = w_query[0], jnp.swapaxes(w_key[0], 1, 2), jnp.swapaxes(w_value[0], 1, 2)
    spans, rows, cols = acts.shape
    n = SUB * rows
    hd = w_query.shape[2]
    kc = w_key.shape[1]
    w_query = w_query.reshape(spans, T, cols, hd)
    V = pltpu.VMEM
    D = pltpu.SemaphoreType.DMA
    scratch = [
        V((2, T, n, cols), BF16), V((SUB, 2, rows), jnp.int32), V((SUB,) + gains.shape, BF16),
        V(w_key.shape, BF16), V(w_value.shape, BF16),
        V((2, T, cols, hd + 2 * kc), BF16), V(head_grads.shape, BF16), V(grads_in.shape, BF16),
        V((2, n, 128), F32), V((2, n, 128), F32), V((2, n, hd + 2 * kc), F32), V((2, n, 128), F32),
        V((2, 2, hd, n), BF16), V((2, 2, hd, n), BF16), V((T - 1, 2, 2, kc, n), BF16),
        V((2, 8, n), F32), V((2, T - 1, 8, n), F32), V((2, 8, n), F32), V((2, SUB - 1, 8, n), F32),
        V((2, T, 2, 2, rows, cols), BF16), V((2, T, 2, rows, cols), BF16),
        V((2, T, rows, cols), BF16), V((2, T, rows, cols), BF16), V((2, T, rows, cols), BF16),
        D((9,)), D((4,)), D((2, 2, 2)), D((1, 2)), D((1, T)), D((2, 1, 1) if T <= 4 else (2, T, 2)), D((2, 3, T)), D((2,)), D((2,)),
        D((2,)), D((2,)), D((2,)), D((2,)), D((2,)), D((2,)), D((2,)), D((2,)),
        D((1,)), D((2, 2, T)), D((1,)), D((2, T)), D((1,)), D((2,)),
    ]

    def body(*refs):
        kernel(sections, T, *refs)

    routed = pl.pallas_call(
        body,
        out_shape=jax.ShapeDtypeStruct((2, T, rows, cols), BF16),
        in_specs=[pl.BlockSpec(memory_space=pl.ANY)] * 8,
        out_specs=pl.BlockSpec(memory_space=pl.ANY),
        scratch_shapes=scratch,
        compiler_params=pltpu.CompilerParams(
            collective_id=0, has_side_effects=True, vmem_limit_bytes=67_000_000
        ),
        name="relay",
    )(acts, grads_in, head_grads, types, gains, w_query, w_key, w_value)
    return jnp.sum(routed.astype(F32), axis=1).astype(BF16)[None]


def solution(mesh):
    sections = mesh.shape["section"] // SUB

    def run(*args):
        return per_device(sections, *args)

    return jax.shard_map(
        run,
        mesh=mesh,
        in_specs=(
            P("section", None, None, "tensor"),
            P("section", None, None, "tensor"),
            P("section", None, None, "tensor"),
            P("section", None, None),
            P("section", None, None, None),
            P("section", None, None, "tensor"),
            P("section", None, None, "tensor"),
            P("section", None, None, "tensor"),
        ),
        out_specs=P("section", None, None, "tensor"),
        check_vma=False,
    )
```
